512 devices in a mesh: crop: 4 (over x_lo, core), row: 128 (over y, x_hi, z).
Axes of the slice: x: 4 (x_hi: 2, x_lo: 2; x = x_hi * 2 + x_lo), y: 8, z: 8, core: 2. Of those that a mesh axis runs over, the one named last changes fastest.
Arguments:
- pair: bfloat16 [1024, 256, 128], P(('crop', 'row')), parts along dimension 0, may hold values from -6 to 6
- out_grad: bfloat16 [1024, 256, 128], P('crop', 'row'), parts along dimension 0, may hold values from -6 to 6
- w_qkvg: bfloat16 [128, 512], replicated, may hold values from -0.5 to 0.5
- w_out: bfloat16 [128, 128], replicated, may hold values from -0.5 to 0.5
- w_bias: bfloat16 [128, 4], replicated, may hold values from -32 to 32
- gain: float32 [128], replicated, may hold values from 0.1 to 1.9
Outputs:
- d_pair: bfloat16 [1024, 256, 128], P(('crop', 'row')), parts along dimension 0
- d_qkvg: float32 [512, 512], P('crop'), parts along dimension 0
- d_wout: float32 [512, 128], P('crop'), parts along dimension 0
- d_wbias: float32 [512, 4], P('crop'), parts along dimension 0
- d_gain: float32 [512], P('crop'), parts along dimension 0
The draws below stay inside these ranges and needn't reach their ends.
There are 4 independent parts, one for each index of `crop`. The reference program is written for one: setup_inputs(seed, part) draws one part's arguments, and reference() takes and returns one part's arrays. A program takes and returns all parts, laid end to end along the dimension named above; an argument that names none is the same for every part. Nothing has to cross between parts.
All inputs are finite; a program needn't handle non-finite values.
Results may differ from the reference program's by a relative error of at most 0.014.
The reference program's roundings to bfloat16 on the way count: a program that leaves them out, or rounds other values in their place, can miss the bound.
Values may be sent and summed in bfloat16 or wider, within the bound.
No kernel may reach another device: no remote copies, remote signals or barrier semaphores. Data moves between devices by JAX's collectives and lax.ppermute only.
A program may use at most 64 MiB of HBM per device.

```python
import jax
import jax.numpy as jnp
from jax import lax

C = 128
H = 4
DH = 32
N = 256


def draw_w_bias(key, part):
    base = jax.random.normal(key, (C, H), jnp.float32)
    weights = base * 1.5 * C ** (-0.5)
    return jnp.clip(weights, -32.0, 32.0).astype(jnp.bfloat16)


def block_scale(own_key, shape, split, low, largest):
    def one(position, shards_of):
        steps = jax.random.uniform(jax.random.fold_in(jax.random.fold_in(own_key, 6), position), (shards_of,), jnp.float32, low / len(split), largest / len(split))
        return jnp.repeat(jnp.exp(steps), shape[position] // shards_of).reshape((-1,) + (1,) * (len(shape) - position - 1))

    level = one(*split[0])
    for cut in split[1:]:
        level = level * one(*cut)
    return level


def scatter_about(own_key, extent, scale, reach, pieces=(), held_as=jnp.bfloat16):
    result = jax.random.normal(own_key, extent, jnp.float32) * scale
    if len(pieces) > 0:
        result = block_scale(own_key, extent, pieces, -0.22, 0.18) * result
    return jnp.clip(result, min=-reach, max=reach).astype(held_as)


def setup_inputs(seed: int = 0, part: int = 0) -> dict:
    key_list = jax.random.split(jax.random.key(seed), 7)
    part_splits = jax.random.split(jax.random.fold_in(key_list[6], part), 7)
    return {
        "pair": scatter_about(part_splits[0], (N, N, C), 1.0, 6.0, ((0, 128),)),
        "out_grad": scatter_about(part_splits[1], (N, N, C), 1.0, 6.0, ((1, 128),)),
        "w_qkvg": scatter_about(key_list[2], (C, 4 * C), C ** -0.5, 0.5),
        "w_out": scatter_about(key_list[3], (C, C), C ** -0.5, 0.5),
        "w_bias": draw_w_bias(jax.random.fold_in(key_list[6], 71), part),
        "gain": jnp.clip(1.0 + 0.18 * jax.random.normal(key_list[5], (C,), jnp.float32), 0.1, 1.9),
    }


EPSILON = 1e-05

def normalize(pair, gain):
    values = pair.astype(jnp.float32)
    center = lax.optimization_barrier(jnp.mean(values, axis=-1, keepdims=True))
    spread = lax.optimization_barrier(jnp.mean(jnp.square(values - center), axis=-1, keepdims=True))
    inv_std = lax.rsqrt(spread + EPSILON)
    normed = (values - center) * inv_std
    return ((normed * gain).astype(jnp.bfloat16), normed, inv_std)

def column_grad(tokens, grads, w_qkvg, w_out, bias, scale):
    width = w_out.shape[0]
    heads = bias.shape[0]
    size = width // heads
    count = tokens.shape[0]
    proj = jnp.dot(tokens, w_qkvg, preferred_element_type=jnp.float32)
    queries = proj[:, :width].astype(jnp.bfloat16).reshape(count, heads, size).astype(jnp.float32)
    keys = proj[:, width:2 * width].astype(jnp.bfloat16).reshape(count, heads, size).astype(jnp.float32)
    values = proj[:, 2 * width:3 * width].astype(jnp.bfloat16).reshape(count, heads, size).astype(jnp.float32)
    gate = jax.nn.sigmoid(proj[:, 3 * width:]).reshape(count, heads, size)
    scores = jnp.einsum('khd,ihd->hki', keys, queries) * scale + bias.astype(jnp.float32)
    probs = jax.nn.softmax(scores, axis=1)
    probs_b = probs.astype(jnp.bfloat16).astype(jnp.float32)
    attended = jnp.einsum('hki,khd->ihd', probs_b, values)
    mixed = (gate * attended).astype(jnp.bfloat16).reshape(count, width)
    d_mixed = jnp.dot(grads, w_out.T, preferred_element_type=jnp.float32).reshape(count, heads, size)
    part_wout = jnp.dot(mixed.T, grads, preferred_element_type=jnp.float32)
    d_gate = d_mixed * attended * gate * (1.0 - gate)
    d_att = (d_mixed * gate).astype(jnp.bfloat16).astype(jnp.float32)
    d_values = jnp.einsum('hki,ihd->khd', probs_b, d_att)
    d_probs = jnp.einsum('ihd,khd->hki', d_att, values)
    delta = lax.optimization_barrier(jnp.sum(d_att * attended, axis=-1))
    d_scores = (probs * (d_probs - delta.T[:, None, :])).astype(jnp.bfloat16)
    d_sf = d_scores.astype(jnp.float32)
    d_queries = jnp.einsum('hki,khd->ihd', d_sf, keys) * scale
    d_keys = jnp.einsum('hki,ihd->khd', d_sf, queries) * scale
    d_proj = jnp.concatenate([d_queries.reshape(count, width), d_keys.reshape(count, width), d_values.reshape(count, width), d_gate.reshape(count, width)], axis=1).astype(jnp.bfloat16)
    part_qkvg = jnp.dot(tokens.T, d_proj, preferred_element_type=jnp.float32)
    d_tokens = jnp.dot(d_proj, w_qkvg.T, preferred_element_type=jnp.float32).astype(jnp.bfloat16)
    return (d_tokens, d_scores, part_qkvg, part_wout)

def reference(pair, out_grad, w_qkvg, w_out, w_bias, gain):
    normed_b, normed, inv_std = normalize(pair, gain)
    bias = jnp.einsum('abc,ch->hab', normed_b.astype(jnp.float32), w_bias.astype(jnp.float32)).astype(jnp.bfloat16)
    scale = DH ** (-0.5)
    width = w_out.shape[0]
    heads = w_bias.shape[1]
    length = pair.shape[1]
    inv_count = 1.0 / length

    def step(carry, column):
        d_bias, d_qkvg, d_wout = carry
        tokens = lax.dynamic_index_in_dim(normed_b, column, 1, keepdims=False)
        grads = lax.dynamic_index_in_dim(out_grad, column, 1, keepdims=False)
        d_tokens, d_scores, part_qkvg, part_wout = column_grad(tokens, grads, w_qkvg, w_out, bias, scale)
        return ((d_bias + d_scores.astype(jnp.float32), d_qkvg + part_qkvg, d_wout + part_wout), d_tokens)
    start = (jnp.zeros((heads, length, length), jnp.float32), jnp.zeros((width, 4 * width), jnp.float32), jnp.zeros((width, width), jnp.float32))
    (d_bias, d_qkvg, d_wout), d_cols = lax.scan(step, start, jnp.arange(length, dtype=jnp.int32))
    d_att_x = jnp.swapaxes(d_cols, 0, 1)
    d_bias_x = jnp.einsum('hab,ch->abc', d_bias, w_bias.astype(jnp.float32), precision=lax.Precision.HIGHEST).astype(jnp.bfloat16)
    d_wbias = jnp.einsum('abc,hab->ch', normed_b.astype(jnp.float32), d_bias, precision=lax.Precision.HIGHEST)
    d_xn = d_att_x.astype(jnp.float32) + d_bias_x.astype(jnp.float32)
    d_gain = lax.optimization_barrier(jnp.sum(d_xn * normed, axis=(0, 1)))
    scaled = d_xn * gain
    d_pair = (inv_std * (scaled - lax.optimization_barrier(jnp.mean(scaled, axis=-1, keepdims=True)) - normed * lax.optimization_barrier(jnp.mean(scaled * normed, axis=-1, keepdims=True)))).astype(jnp.bfloat16)
    return (d_pair, d_qkvg * inv_count, d_wout * inv_count, d_wbias * inv_count, d_gain * inv_count)
```

```python
import jax
import jax.numpy as jnp
from jax import lax
from jax.experimental import pallas as pl
from jax.experimental.pallas import tpu as pltpu
from jax.sharding import Mesh
from jax.sharding import PartitionSpec as P

DH = 32
H = 4
C = 128
N = 256
DEV = 128
SCALE = DH ** (-0.5)
ROW = ("row_0", "row_1", "row_2")
CROP_ROW = ("crop", "row_0", "row_1", "row_2")
EPSILON = 1e-05
F32 = jnp.float32
BF16 = jnp.bfloat16


def dot(a, b, ca=1, cb=0):
    return lax.dot_general(a, b, (((ca,), (cb,)), ((), ())), preferred_element_type=F32)


def normalize(pair, gain):
    values = pair.astype(F32)
    center = jnp.mean(values, axis=-1, keepdims=True)
    spread = jnp.mean(jnp.square(values - center), axis=-1, keepdims=True)
    inv_std = lax.rsqrt(spread + EPSILON)
    normed = (values - center) * inv_std
    return ((normed * gain).astype(BF16), normed, inv_std)


def attention_kernel(cols_ref, grad_ref, w_ref, wt_ref, wout_ref, out_ref, dbias_ref):
    lane = lax.broadcasted_iota(jnp.int32, (N, C), 1) // DH
    zero = jnp.zeros((N, C), BF16)
    d_w = d_wout = None
    for c in range(2):
        tokens = jnp.concatenate([cols_ref[16 + c], cols_ref[18 + c]], axis=0)
        grads = grad_ref[c]
        proj = dot(tokens, w_ref[:, : 3 * C]).astype(BF16)
        q, k, v = proj[:, :C], proj[:, C : 2 * C], proj[:, 2 * C :]
        proj_t = dot(wt_ref[...], tokens, 1, 1)
        q_t = proj_t[:C].astype(BF16)
        k_t = proj_t[C : 2 * C].astype(BF16)
        v_t = proj_t[2 * C : 3 * C].astype(BF16)
        gate_t = jax.nn.sigmoid(proj_t[3 * C :])
        d_mixed_t = dot(wout_ref[...], grads, 1, 1)
        d_att_t = (d_mixed_t * gate_t).astype(BF16)
        d_att = d_att_t.T
        att_t, dq_t = [], []
        d_k = d_v = None
        for h in range(H):
            own = lane == h
            rows = slice(h * DH, (h + 1) * DH)
            bias = jnp.concatenate(
                [
                    jnp.concatenate([cols_ref[4 * h + 2 * r], cols_ref[4 * h + 2 * r + 1]], axis=1)
                    for r in range(2)
                ],
                axis=0,
            ).astype(F32)
            s = dot(jnp.where(own, k, zero), q_t) * SCALE + bias
            e = jnp.exp(s - jnp.max(s, axis=0, keepdims=True))
            probs = e * (1.0 / jnp.sum(e, axis=0, keepdims=True))
            probs_b = probs.astype(BF16)
            att_h = dot(v_t[rows], probs_b)
            delta = jnp.sum(d_att_t[rows].astype(F32) * att_h, axis=0, keepdims=True)
            d_probs = dot(jnp.where(own, v, zero), d_att_t)
            d_s = (probs * (d_probs - delta)).astype(BF16)
            att_t.append(att_h)
            dq_t.append(dot(k_t[rows], d_s))
            dk_h = dot(d_s, jnp.where(own, q, zero))
            dv_h = dot(probs_b, jnp.where(own, d_att, zero))
            d_k = dk_h if d_k is None else d_k + dk_h
            d_v = dv_h if d_v is None else d_v + dv_h
            if c == 0:
                dbias_ref[h] = d_s
            else:
                total = (dbias_ref[h].astype(F32) + d_s.astype(F32)).astype(BF16)
                for r in range(2):
                    for half in range(2):
                        out_ref[4 * h + 2 * r + half] = total[
                            r * 128 : (r + 1) * 128, half * 128 : (half + 1) * 128
                        ]
        att_t = jnp.concatenate(att_t, axis=0)
        mixed_t = (gate_t * att_t).astype(BF16)
        d_gate_t = (d_mixed_t * att_t * gate_t * (1.0 - gate_t)).astype(BF16)
        d_q_t = (jnp.concatenate(dq_t, axis=0) * SCALE).astype(BF16)
        d_proj = jnp.concatenate(
            [d_q_t.T, (d_k * SCALE).astype(BF16), d_v.astype(BF16), d_gate_t.T], axis=1
        )
        part_wout = dot(mixed_t, grads)
        part_w = dot(tokens, d_proj, 0, 0)
        d_w = part_w if d_w is None else d_w + part_w
        d_wout = part_wout if d_wout is None else d_wout + part_wout
        d_tokens = dot(d_proj, wt_ref[...]).astype(BF16)
        out_ref[16 + c] = d_tokens[:128]
        out_ref[18 + c] = d_tokens[128:]
    for block in range(4):
        out_ref[20 + block] = d_w[:, block * C : (block + 1) * C].astype(BF16)
    out_ref[24] = d_wout.astype(BF16)


def attention(cols, grads, w, w_t, w_out):
    return pl.pallas_call(
        attention_kernel,
        out_shape=jax.ShapeDtypeStruct((25, DEV, C), BF16),
        scratch_shapes=[pltpu.VMEM((H, N, N), BF16)],
        cost_estimate=pl.CostEstimate(
            flops=900_000_000, bytes_accessed=3_000_000, transcendentals=600_000
        ),
    )(cols, grads, w, w_t, w_out)


def exchanged(blocks):
    return lax.all_to_all(blocks, ROW, split_axis=0, concat_axis=0, tiled=True)


def per_device(pair, out_grad, w_qkvg, w_out, w_bias, gain):
    pair = pair.reshape(2, 128, 2, C).transpose(0, 2, 1, 3)
    xn, normed, inv_std = normalize(pair, gain)
    bias = jnp.einsum("rcpd,dh->hrcp", xn, w_bias, preferred_element_type=F32).astype(BF16)
    sent = jnp.concatenate(
        [
            jnp.broadcast_to(bias.reshape(1, 16, 128), (DEV, 16, 128)),
            xn.reshape(4, 128, C).transpose(1, 0, 2),
        ],
        axis=1,
    )
    cols = exchanged(sent).transpose(1, 0, 2)
    grads = out_grad.reshape(128, 2, 2, C).transpose(2, 1, 0, 3).reshape(2, N, C)
    planes = attention(cols, grads, w_qkvg, w_qkvg.T, w_out)
    back = exchanged(planes.transpose(1, 0, 2))
    summed = jnp.sum(
        jnp.concatenate([back[:, :16], back[:, 20:]], axis=1).astype(F32), axis=0
    )
    d_bias = summed[:16].reshape(H, 2, 2, 128)
    d_att_x = back[:, 16:20].transpose(1, 0, 2).reshape(2, 2, 128, C)
    d_bias_x = jnp.einsum(
        "hrcp,dh->rcpd", d_bias, w_bias.astype(F32), precision=lax.Precision.HIGHEST
    ).astype(BF16)
    d_wbias = jnp.einsum(
        "rcpd,hrcp->hd", xn.astype(F32), d_bias, precision=lax.Precision.HIGHEST
    )
    d_xn = d_att_x.astype(F32) + d_bias_x.astype(F32)
    d_gain = jnp.sum(d_xn * normed, axis=(0, 1, 2))
    scaled = d_xn * gain
    d_pair = (
        inv_std
        * (
            scaled
            - jnp.mean(scaled, axis=-1, keepdims=True)
            - normed * jnp.mean(scaled * normed, axis=-1, keepdims=True)
        )
    ).astype(BF16)
    d_pair = d_pair.transpose(0, 2, 1, 3).reshape(2, N, C)
    own = jnp.concatenate([summed[16:], d_wbias, d_gain[None]], axis=0).astype(BF16)
    last = exchanged(jnp.broadcast_to(own[None], (DEV, 10, C))).astype(F32) * (1.0 / N)
    small = jnp.sum(last[:, 5:], axis=0)
    return (
        d_pair,
        last[:, :4].reshape(C, 4 * C),
        last[:, 4],
        small[:4].T,
        small[4],
    )


def solution(mesh):
    split = Mesh(
        mesh.devices.reshape(mesh.shape["crop"], 8, 2, 8), ("crop", "row_0", "row_1", "row_2")
    )
    placed = (P(CROP_ROW, None, None), P("crop", ROW, None), P(), P(), P(), P())
    return jax.shard_map(
        per_device,
        mesh=split,
        in_specs=placed,
        out_specs=(
            P(CROP_ROW, None, None),
            P("crop", None),
            P("crop", None),
            P("crop", None),
            P("crop"),
        ),
        check_vma=False,
    )
```

```python
import jax
import jax.numpy as jnp
from jax import lax
from jax.experimental import pallas as pl
from jax.experimental.pallas import tpu as pltpu
from jax.sharding import Mesh
from jax.sharding import PartitionSpec as P

DH = 32
H = 4
C = 128
N = 256
DEV = 128
SCALE = DH ** (-0.5)
ROW = ("row_0", "row_1", "row_2")
CROP_ROW = ("crop", "row_0", "row_1", "row_2")
EPSILON = 1e-05
F32 = jnp.float32
BF16 = jnp.bfloat16


def dot(a, b, ca=1, cb=0):
    return lax.dot_general(a, b, (((ca,), (cb,)), ((), ())), preferred_element_type=F32)


def normalize(pair, gain):
    values = pair.astype(F32)
    center = jnp.mean(values, axis=-1, keepdims=True)
    spread = jnp.mean(jnp.square(values - center), axis=-1, keepdims=True)
    inv_std = lax.rsqrt(spread + EPSILON)
    normed = (values - center) * inv_std
    return ((normed * gain).astype(BF16), normed, inv_std)


def attention_kernel(cols_ref, grad_ref, w_ref, wt_ref, wout_ref, out_ref, dbias_ref):
    lane = lax.broadcasted_iota(jnp.int32, (N, C), 1) // DH
    zero = jnp.zeros((N, C), BF16)
    d_w = d_wout = None
    for c in range(2):
        tokens = jnp.concatenate([cols_ref[16 + c], cols_ref[18 + c]], axis=0)
        grads = grad_ref[c]
        proj = dot(tokens, w_ref[:, : 3 * C]).astype(BF16)
        q, k, v = proj[:, :C], proj[:, C : 2 * C], proj[:, 2 * C :]
        proj_t = dot(wt_ref[...], tokens, 1, 1)
        q_t = proj_t[:C].astype(BF16)
        k_t = proj_t[C : 2 * C].astype(BF16)
        v_t = proj_t[2 * C : 3 * C].astype(BF16)
        gate_t = jax.nn.sigmoid(proj_t[3 * C :])
        d_mixed_t = dot(wout_ref[...], grads, 1, 1)
        d_att_t = (d_mixed_t * gate_t).astype(BF16)
        d_att = d_att_t.T
        att_t, dq_t = [], []
        d_k = d_v = None
        for h in range(H):
            own = lane == h
            rows = slice(h * DH, (h + 1) * DH)
            bias = jnp.concatenate(
                [
                    jnp.concatenate([cols_ref[4 * h + 2 * r], cols_ref[4 * h + 2 * r + 1]], axis=1)
                    for r in range(2)
                ],
                axis=0,
            ).astype(F32)
            s = dot(jnp.where(own, k, zero), q_t) * SCALE + bias
            e = jnp.exp(s - jnp.max(s, axis=0, keepdims=True))
            probs = e * (1.0 / jnp.sum(e, axis=0, keepdims=True))
            probs_b = probs.astype(BF16)
            att_h = dot(v_t[rows], probs_b)
            delta = jnp.sum(d_att_t[rows].astype(F32) * att_h, axis=0, keepdims=True)
            d_probs = dot(jnp.where(own, v, zero), d_att_t)
            d_s = (probs * (d_probs - delta)).astype(BF16)
            att_t.append(att_h)
            dq_t.append(dot(k_t[rows], d_s))
            dk_h = dot(d_s, jnp.where(own, q, zero))
            dv_h = dot(probs_b, jnp.where(own, d_att, zero))
            d_k = dk_h if d_k is None else d_k + dk_h
            d_v = dv_h if d_v is None else d_v + dv_h
            if c == 0:
                dbias_ref[h] = d_s
            else:
                total = (dbias_ref[h].astype(F32) + d_s.astype(F32)).astype(BF16)
                for r in range(2):
                    for half in range(2):
                        out_ref[4 * h + 2 * r + half] = total[
                            r * 128 : (r + 1) * 128, half * 128 : (half + 1) * 128
                        ]
        att_t = jnp.concatenate(att_t, axis=0)
        mixed_t = (gate_t * att_t).astype(BF16)
        d_gate_t = (d_mixed_t * att_t * gate_t * (1.0 - gate_t)).astype(BF16)
        d_q_t = (jnp.concatenate(dq_t, axis=0) * SCALE).astype(BF16)
        d_proj = jnp.concatenate(
            [d_q_t.T, (d_k * SCALE).astype(BF16), d_v.astype(BF16), d_gate_t.T], axis=1
        )
        part_wout = dot(mixed_t, grads)
        part_w = dot(tokens, d_proj, 0, 0)
        d_w = part_w if d_w is None else d_w + part_w
        d_wout = part_wout if d_wout is None else d_wout + part_wout
        d_tokens = dot(d_proj, wt_ref[...]).astype(BF16)
        out_ref[16 + c] = d_tokens[:128]
        out_ref[18 + c] = d_tokens[128:]
    for block in range(4):
        out_ref[20 + block] = d_w[:, block * C : (block + 1) * C].astype(BF16)
    out_ref[24] = d_wout.astype(BF16)


def attention(cols, grads, w, w_t, w_out):
    return pl.pallas_call(
        attention_kernel,
        out_shape=jax.ShapeDtypeStruct((25, DEV, C), BF16),
        scratch_shapes=[pltpu.VMEM((H, N, N), BF16)],
        cost_estimate=pl.CostEstimate(
            flops=900_000_000, bytes_accessed=3_000_000, transcendentals=600_000
        ),
    )(cols, grads, w, w_t, w_out)


def exchanged(blocks, group):
    rows = blocks.shape[1]
    spare = -rows % group
    if spare:
        blocks = jnp.concatenate([blocks, jnp.zeros((DEV, spare, C), blocks.dtype)], axis=1)
    blocks = blocks.reshape(DEV, -1, group, C)
    moved = lax.all_to_all(blocks, ROW, split_axis=0, concat_axis=0, tiled=True)
    return moved.reshape(DEV, -1, C)[:, :rows]


def per_device(pair, out_grad, w_qkvg, w_out, w_bias, gain):
    pair = pair.reshape(2, 128, 2, C).transpose(0, 2, 1, 3)
    xn, normed, inv_std = normalize(pair, gain)
    bias = jnp.einsum("rcpd,dh->hrcp", xn, w_bias, preferred_element_type=F32).astype(BF16)
    sent = jnp.concatenate(
        [
            jnp.broadcast_to(bias.reshape(1, 16, 128), (DEV, 16, 128)),
            xn.reshape(4, 128, C).transpose(1, 0, 2),
        ],
        axis=1,
    )
    cols = exchanged(sent, 4).transpose(1, 0, 2)
    grads = out_grad.reshape(128, 2, 2, C).transpose(2, 1, 0, 3).reshape(2, N, C)
    planes = attention(cols, grads, w_qkvg, w_qkvg.T, w_out)
    back = exchanged(planes.transpose(1, 0, 2), 2)
    summed = jnp.sum(
        jnp.concatenate([back[:, :16], back[:, 20:]], axis=1).astype(F32), axis=0
    )
    d_bias = summed[:16].reshape(H, 2, 2, 128)
    d_att_x = back[:, 16:20].transpose(1, 0, 2).reshape(2, 2, 128, C)
    d_bias_x = jnp.einsum(
        "hrcp,dh->rcpd", d_bias, w_bias.astype(F32), precision=lax.Precision.HIGHEST
    ).astype(BF16)
    d_wbias = jnp.einsum(
        "rcpd,hrcp->hd", xn.astype(F32), d_bias, precision=lax.Precision.HIGHEST
    )
    d_xn = d_att_x.astype(F32) + d_bias_x.astype(F32)
    d_gain = jnp.sum(d_xn * normed, axis=(0, 1, 2))
    scaled = d_xn * gain
    d_pair = (
        inv_std
        * (
            scaled
            - jnp.mean(scaled, axis=-1, keepdims=True)
            - normed * jnp.mean(scaled * normed, axis=-1, keepdims=True)
        )
    ).astype(BF16)
    d_pair = d_pair.transpose(0, 2, 1, 3).reshape(2, N, C)
    own = jnp.concatenate([summed[16:], d_wbias, d_gain[None]], axis=0).astype(BF16)
    last = exchanged(jnp.broadcast_to(own[None], (DEV, 10, C)), 2).astype(F32) * (1.0 / N)
    small = jnp.sum(last[:, 5:], axis=0)
    return (
        d_pair,
        last[:, :4].reshape(C, 4 * C),
        last[:, 4],
        small[:4].T,
        small[4],
    )


def solution(mesh):
    split = Mesh(
        mesh.devices.reshape(mesh.shape["crop"], 8, 2, 8), ("crop", "row_0", "row_1", "row_2")
    )
    placed = (P(CROP_ROW, None, None), P("crop", ROW, None), P(), P(), P(), P())
    return jax.shard_map(
        per_device,
        mesh=split,
        in_specs=placed,
        out_specs=(
            P(CROP_ROW, None, None),
            P("crop", None),
            P("crop", None),
            P("crop", None),
            P("crop"),
        ),
        check_vma=False,
    )
```

```python
import jax
import jax.numpy as jnp
from jax import lax
from jax.experimental import pallas as pl
from jax.experimental.pallas import tpu as pltpu
from jax.sharding import Mesh
from jax.sharding import PartitionSpec as P

DH = 32
H = 4
C = 128
N = 256
DEV = 128
SCALE = DH ** (-0.5)
ROW = ("row_0", "row_1", "row_2")
CROP_ROW = ("crop", "row_0", "row_1", "row_2")
EPSILON = 1e-05
LOG2E = 1.4426950408889634
F32 = jnp.float32
BF16 = jnp.bfloat16


def dot(a, b, ca=1, cb=0):
    return lax.dot_general(a, b, (((ca,), (cb,)), ((), ())), preferred_element_type=F32)


def normalize(pair, gain):
    values = pair.astype(F32)
    center = jnp.mean(values, axis=-1, keepdims=True)
    spread = jnp.mean(jnp.square(values - center), axis=-1, keepdims=True)
    inv_std = lax.rsqrt(spread + EPSILON)
    normed = (values - center) * inv_std
    return ((normed * gain).astype(BF16), normed, inv_std)


def attention_kernel(cols_ref, grad_ref, w_ref, wt_ref, wout_ref, out_ref):
    lane = lax.broadcasted_iota(jnp.int32, (N, C), 1) // DH
    zero = jnp.zeros((N, C), BF16)

    def prepare(c):
        tokens = jnp.concatenate([cols_ref[16 + c], cols_ref[18 + c]], axis=0)
        grads = grad_ref[c]
        proj = dot(tokens, w_ref[:, : 3 * C]).astype(BF16)
        proj_t = dot(wt_ref[...], tokens, 1, 1)
        gate_t = jax.nn.sigmoid(proj_t[3 * C :])
        d_mixed_t = dot(wout_ref[...], grads, 1, 1)
        d_att_t = (d_mixed_t * gate_t).astype(BF16)
        return dict(
            tokens=tokens,
            grads=grads,
            q=proj[:, :C],
            k=proj[:, C : 2 * C],
            v=proj[:, 2 * C :],
            q_t=proj_t[:C].astype(BF16),
            k_t=proj_t[C : 2 * C].astype(BF16),
            v_t=proj_t[2 * C : 3 * C].astype(BF16),
            gate_t=gate_t,
            d_mixed_t=d_mixed_t,
            d_att_t=d_att_t,
            d_att=d_att_t.T,
            att_h=[],
            dq_h=[],
            d_k=None,
            d_v=None,
        )

    def raw(col, h):
        rows = slice(h * DH, (h + 1) * DH)
        s = dot(col["k"][:, rows], col["q_t"][rows])
        d_probs = dot(col["v"][:, rows], col["d_att_t"][rows])
        return s, d_probs

    def head(col, h, bias, s, d_probs):
        own = lane == h
        rows = slice(h * DH, (h + 1) * DH)
        s = s * (SCALE * LOG2E) + bias
        e = jnp.exp2(s - jnp.max(s, axis=0, keepdims=True))
        probs = e * (1.0 / jnp.sum(e, axis=0, keepdims=True))
        probs_b = probs.astype(BF16)
        att_h = dot(col["v_t"][rows], probs_b)
        delta = jnp.sum(col["d_att_t"][rows].astype(F32) * att_h, axis=0, keepdims=True)
        d_s = probs * (d_probs - delta)
        d_sb = d_s.astype(BF16)
        col["att_h"].append(att_h)
        col["dq_h"].append(dot(col["k_t"][rows], d_sb))
        dk_h = dot(d_sb, jnp.where(own, col["q"], zero))
        dv_h = dot(probs_b, jnp.where(own, col["d_att"], zero))
        col["d_k"] = dk_h if h == 0 else col["d_k"] + dk_h
        col["d_v"] = dv_h if h == 0 else col["d_v"] + dv_h
        return d_s

    def finish(col):
        att_t = jnp.concatenate(col["att_h"], axis=0)
        gate_t = col["gate_t"]
        mixed_t = (gate_t * att_t).astype(BF16)
        d_gate_t = (col["d_mixed_t"] * att_t * gate_t * (1.0 - gate_t)).astype(BF16)
        d_q_t = (jnp.concatenate(col["dq_h"], axis=0) * SCALE).astype(BF16)
        d_proj = jnp.concatenate(
            [d_q_t.T, (col["d_k"] * SCALE).astype(BF16), col["d_v"].astype(BF16), d_gate_t.T],
            axis=1,
        )
        d_tokens = dot(d_proj, wt_ref[...]).astype(BF16)
        return dot(col["tokens"], d_proj, 0, 0), dot(mixed_t, col["grads"]), d_tokens

    def bias_of(h):
        return (
            jnp.concatenate(
                [
                    jnp.concatenate([cols_ref[4 * h + 2 * r], cols_ref[4 * h + 2 * r + 1]], axis=1)
                    for r in range(2)
                ],
                axis=0,
            ).astype(F32)
            * LOG2E
        )

    cols = [prepare(0), prepare(1)]
    order = [(h, c) for h in range(H) for c in range(2)]
    ahead = raw(cols[0], 0)
    for t, (h, c) in enumerate(order):
        s, d_probs = ahead
        if t + 1 < len(order):
            ahead = raw(cols[order[t + 1][1]], order[t + 1][0])
        if c == 0:
            bias = bias_of(h)
        d_s = head(cols[c], h, bias, s, d_probs)
        if c == 0:
            first = d_s
        else:
            total = (first + d_s).astype(BF16)
            for r in range(2):
                for half in range(2):
                    out_ref[4 * h + 2 * r + half] = total[
                        r * 128 : (r + 1) * 128, half * 128 : (half + 1) * 128
                    ]
    d_w, d_wout = 0.0, 0.0
    for c in range(2):
        part_w, part_wout, d_tokens = finish(cols[c])
        d_w, d_wout = d_w + part_w, d_wout + part_wout
        out_ref[16 + c] = d_tokens[:128]
        out_ref[18 + c] = d_tokens[128:]
    for block in range(4):
        out_ref[20 + block] = d_w[:, block * C : (block + 1) * C].astype(BF16)
    out_ref[24] = d_wout.astype(BF16)
    out_ref[25] = jnp.zeros((DEV, C), BF16)


def vmem(count):
    return [pl.BlockSpec(memory_space=pltpu.VMEM)] * count


def attention(cols, grads, w, w_t, w_out):
    return pl.pallas_call(
        attention_kernel,
        out_shape=jax.ShapeDtypeStruct((26, DEV, C), BF16),
        in_specs=vmem(5),
        out_specs=vmem(1)[0],
        compiler_params=pltpu.CompilerParams(
            vmem_limit_bytes=24 << 20
        ),
        cost_estimate=pl.CostEstimate(
            flops=900_000_000, bytes_accessed=3_000_000, transcendentals=600_000
        ),
    )(cols, grads, w, w_t, w_out)


def totals_kernel(planes_ref, w_ref, wout_ref, wbias_ref, gain_ref):
    scale = 1.0 / N
    for block in range(4):
        w_ref[:, block * C : (block + 1) * C] = planes_ref[block].astype(F32) * scale
    wout_ref[...] = planes_ref[4].astype(F32) * scale
    for h in range(H):
        wbias_ref[h : h + 1] = (
            jnp.sum(planes_ref[5 + h].astype(F32), axis=0, keepdims=True) * scale
        )
    gain_ref[...] = jnp.sum(planes_ref[9].astype(F32), axis=0, keepdims=True) * scale


def totals(planes):
    return pl.pallas_call(
        totals_kernel,
        out_shape=(
            jax.ShapeDtypeStruct((C, 4 * C), F32),
            jax.ShapeDtypeStruct((C, C), F32),
            jax.ShapeDtypeStruct((H, C), F32),
            jax.ShapeDtypeStruct((1, C), F32),
        ),
        in_specs=vmem(1),
        out_specs=tuple(vmem(4)),
        compiler_params=pltpu.CompilerParams(vmem_limit_bytes=8 << 20),
    )(planes)


def exchanged(blocks, group):
    rows = blocks.shape[1]
    spare = -rows % group
    if spare:
        blocks = jnp.concatenate([blocks, jnp.zeros((DEV, spare, C), blocks.dtype)], axis=1)
    blocks = blocks.reshape(DEV, -1, group, C)
    moved = lax.all_to_all(blocks, ROW, split_axis=0, concat_axis=0, tiled=True)
    return moved.reshape(DEV, -1, C)[:, :rows]


def per_device(pair, out_grad, w_qkvg, w_out, w_bias, gain):
    pair = pair.reshape(2, 128, 2, C).transpose(0, 2, 1, 3)
    xn, normed, inv_std = normalize(pair, gain)
    bias = jnp.einsum("rcpd,dh->hrcp", xn, w_bias, preferred_element_type=F32).astype(BF16)
    sent = jnp.concatenate(
        [
            jnp.broadcast_to(bias.reshape(1, 16, 128), (DEV, 16, 128)),
            xn.reshape(4, 128, C).transpose(1, 0, 2),
        ],
        axis=1,
    )
    cols = exchanged(sent, 4).transpose(1, 0, 2)
    grads = out_grad.reshape(128, 2, 2, C).transpose(2, 1, 0, 3).reshape(2, N, C)
    planes = attention(cols, grads, w_qkvg, w_qkvg.T, w_out)
    back = exchanged(planes.transpose(1, 0, 2), 2)
    summed = jnp.sum(
        jnp.concatenate([back[:, :16], back[:, 20:25]], axis=1).astype(F32), axis=0
    )
    d_bias = summed[:16].reshape(H, 2, 2, 128)
    d_att_x = back[:, 16:20].transpose(1, 0, 2).reshape(2, 2, 128, C)
    d_bias_x = jnp.einsum(
        "hrcp,dh->rcpd", d_bias, w_bias.astype(F32), precision=lax.Precision.HIGHEST
    ).astype(BF16)
    d_wbias = jnp.einsum(
        "rcpd,hrcp->hd", xn.astype(F32), d_bias, precision=lax.Precision.HIGHEST
    )
    d_xn = d_att_x.astype(F32) + d_bias_x.astype(F32)
    d_gain = jnp.sum(d_xn * normed, axis=(0, 1, 2))
    scaled = d_xn * gain
    d_pair = (
        inv_std
        * (
            scaled
            - jnp.mean(scaled, axis=-1, keepdims=True)
            - normed * jnp.mean(scaled * normed, axis=-1, keepdims=True)
        )
    ).astype(BF16)
    d_pair = d_pair.transpose(0, 2, 1, 3).reshape(2, N, C)
    own = jnp.concatenate([summed[16:], d_wbias, d_gain[None]], axis=0).astype(BF16)
    last = exchanged(jnp.broadcast_to(own[None], (DEV, 10, C)), 2)
    d_w, d_wout, d_wbias, d_gain = totals(last.transpose(1, 0, 2))
    return d_pair, d_w, d_wout, d_wbias.T, d_gain[0]


def solution(mesh):
    split = Mesh(
        mesh.devices.reshape(mesh.shape["crop"], 8, 2, 8), ("crop", "row_0", "row_1", "row_2")
    )
    placed = (P(CROP_ROW, None, None), P("crop", ROW, None), P(), P(), P(), P())
    return jax.shard_map(
        per_device,
        mesh=split,
        in_specs=placed,
        out_specs=(
            P(CROP_ROW, None, None),
            P("crop", None),
            P("crop", None),
            P("crop", None),
            P("crop"),
        ),
        check_vma=False,
    )
```

```python
import jax
import jax.numpy as jnp
from jax import lax
from jax.experimental import pallas as pl
from jax.experimental.pallas import tpu as pltpu
from jax.sharding import Mesh
from jax.sharding import PartitionSpec as P

DH = 32
H = 4
C = 128
N = 256
DEV = 128
W = 64
SCALE = DH ** (-0.5)
ROW = ("row_0", "row_1", "row_2")
CROP_ROW = ("crop", "row_0", "row_1", "row_2")
EPSILON = 1e-05
LOG2E = 1.4426950408889634
F32 = jnp.float32
BF16 = jnp.bfloat16


def dot(a, b, ca=1, cb=0):
    return lax.dot_general(a, b, (((ca,), (cb,)), ((), ())), preferred_element_type=F32)


def normalize(pair, gain):
    values = pair.astype(F32)
    center = jnp.mean(values, axis=-1, keepdims=True)
    spread = jnp.mean(jnp.square(values - center), axis=-1, keepdims=True)
    inv_std = lax.rsqrt(spread + EPSILON)
    normed = (values - center) * inv_std
    return ((normed * gain).astype(BF16), normed, inv_std)


def attention_kernel(cols_ref, grad_ref, w_ref, wt_ref, wout_ref, out_ref):
    def prepare(t):
        at = 8 + 4 * (t // 2) + t % 2
        tokens = jnp.concatenate([cols_ref[at], cols_ref[at + 2]], axis=0)
        grads = grad_ref[t]
        proj = dot(tokens, w_ref[:, : 3 * W]).astype(BF16)
        proj_t = dot(wt_ref[...], tokens, 1, 1)
        gate_t = jax.nn.sigmoid(proj_t[3 * W :])
        d_mixed_t = dot(wout_ref[...], grads, 1, 1)
        d_att_t = (d_mixed_t * gate_t).astype(BF16)
        return dict(
            tokens=tokens,
            grads=grads,
            q=proj[:, :W],
            k=proj[:, W : 2 * W],
            v=proj[:, 2 * W :],
            q_t=proj_t[:W].astype(BF16),
            k_t=proj_t[W : 2 * W].astype(BF16),
            v_t=proj_t[2 * W : 3 * W].astype(BF16),
            gate_t=gate_t,
            d_mixed_t=d_mixed_t,
            d_att_t=d_att_t,
            d_att=d_att_t.T,
            att_h=[],
            dq_h=[],
            d_k=None,
            d_v=None,
        )

    lane = lax.broadcasted_iota(jnp.int32, (N, W), 1) // DH
    zero = jnp.zeros((N, W), BF16)

    def raw(col, h):
        rows = slice(h * DH, (h + 1) * DH)
        s = dot(col["k"][:, rows], col["q_t"][rows])
        d_probs = dot(col["v"][:, rows], col["d_att_t"][rows])
        return s, d_probs

    def head(col, h, bias, s, d_probs):
        own = lane == h
        rows = slice(h * DH, (h + 1) * DH)
        s = s * (SCALE * LOG2E) + bias
        e = jnp.exp2(s - jnp.max(s, axis=0, keepdims=True))
        probs = e * (1.0 / jnp.sum(e, axis=0, keepdims=True))
        probs_b = probs.astype(BF16)
        att_h = dot(col["v_t"][rows], probs_b)
        delta = jnp.sum(col["d_att_t"][rows].astype(F32) * att_h, axis=0, keepdims=True)
        d_s = probs * (d_probs - delta)
        d_sb = d_s.astype(BF16)
        col["att_h"].append(att_h)
        col["dq_h"].append(dot(col["k_t"][rows], d_sb))
        dk_h = dot(d_sb, jnp.where(own, col["q"], zero))
        dv_h = dot(probs_b, jnp.where(own, col["d_att"], zero))
        col["d_k"] = dk_h if h == 0 else col["d_k"] + dk_h
        col["d_v"] = dv_h if h == 0 else col["d_v"] + dv_h
        return d_s

    def finish(col):
        att_t = jnp.concatenate(col["att_h"], axis=0)
        gate_t = col["gate_t"]
        mixed_t = (gate_t * att_t).astype(BF16)
        d_gate_t = (col["d_mixed_t"] * att_t * gate_t * (1.0 - gate_t)).astype(BF16)
        d_q_t = (jnp.concatenate(col["dq_h"], axis=0) * SCALE).astype(BF16)
        d_proj = jnp.concatenate(
            [d_q_t.T, (col["d_k"] * SCALE).astype(BF16), col["d_v"].astype(BF16), d_gate_t.T],
            axis=1,
        )
        d_tokens = dot(d_proj, wt_ref[...]).astype(BF16)
        return dot(col["tokens"], d_proj, 0, 0), dot(mixed_t, col["grads"]), d_tokens

    def bias_of(h):
        return (
            jnp.concatenate(
                [
                    jnp.concatenate([cols_ref[4 * h + 2 * r], cols_ref[4 * h + 2 * r + 1]], axis=1)
                    for r in range(2)
                ],
                axis=0,
            ).astype(F32)
            * LOG2E
        )

    cols = [prepare(t) for t in range(4)]
    order = [(h, t) for h in range(2) for t in range(4)]
    ahead = raw(cols[0], 0)
    for step, (h, t) in enumerate(order):
        s, d_probs = ahead
        if step + 1 < len(order):
            ahead = raw(cols[order[step + 1][1]], order[step + 1][0])
        if t == 0:
            bias, total = bias_of(h), 0.0
        total = total + head(cols[t], h, bias, s, d_probs)
        if t == 3:
            total = total.astype(BF16)
            for r in range(2):
                for half in range(2):
                    out_ref[4 * h + 2 * r + half] = total[
                        r * 128 : (r + 1) * 128, half * 128 : (half + 1) * 128
                    ]
    d_w, d_wout = 0.0, 0.0
    for t in range(4):
        part_w, part_wout, d_tokens = finish(cols[t])
        d_w, d_wout = d_w + part_w, d_wout + part_wout
        at = 8 + 4 * (t // 2) + t % 2
        out_ref[at] = d_tokens[:128]
        out_ref[at + 2] = d_tokens[128:]
    d_w, d_wout = d_w.astype(BF16), d_wout.astype(BF16)
    for block in range(2):
        out_ref[16 + block] = d_w[:, block * C : (block + 1) * C]
    out_ref[18] = jnp.concatenate(
        [
            jnp.concatenate([d_wout[:, :W], d_wout[:, W:]], axis=0),
            jnp.zeros((DEV, W), BF16),
        ],
        axis=1,
    )
    out_ref[19] = jnp.zeros((DEV, C), BF16)


def vmem(count):
    return [pl.BlockSpec(memory_space=pltpu.VMEM)] * count


def attention(cols, grads, w, w_t, w_out):
    return pl.pallas_call(
        attention_kernel,
        out_shape=jax.ShapeDtypeStruct((20, DEV, C), BF16),
        in_specs=vmem(5),
        out_specs=vmem(1)[0],
        compiler_params=pltpu.CompilerParams(
            vmem_limit_bytes=24 << 20
        ),
        cost_estimate=pl.CostEstimate(
            flops=900_000_000, bytes_accessed=3_000_000, transcendentals=600_000
        ),
    )(cols, grads, w, w_t, w_out)


def totals_kernel(planes_ref, w_ref, wout_ref, wbias_ref, gain_ref):
    scale = 1.0 / N
    for block in range(4):
        at = slice((block % 2) * W, (block % 2 + 1) * W)
        w_ref[:, block * C : (block + 1) * C] = (
            jnp.concatenate(
                [planes_ref[2 * pair + block // 2].astype(F32)[:, at] for pair in range(2)], axis=1
            )
            * scale
        )
    shares = planes_ref[4].astype(F32) * scale
    for pair in range(2):
        own = shares[:, pair * W : (pair + 1) * W]
        wout_ref[pair * W : (pair + 1) * W] = jnp.concatenate([own[:W], own[W:]], axis=1)
    for h in range(H):
        wbias_ref[h : h + 1] = (
            jnp.sum(planes_ref[5 + h].astype(F32), axis=0, keepdims=True) * scale
        )
    gain_ref[...] = jnp.sum(planes_ref[9].astype(F32), axis=0, keepdims=True) * scale


def totals(planes):
    return pl.pallas_call(
        totals_kernel,
        out_shape=(
            jax.ShapeDtypeStruct((C, 4 * C), F32),
            jax.ShapeDtypeStruct((C, C), F32),
            jax.ShapeDtypeStruct((H, C), F32),
            jax.ShapeDtypeStruct((1, C), F32),
        ),
        in_specs=vmem(1),
        out_specs=tuple(vmem(4)),
        compiler_params=pltpu.CompilerParams(vmem_limit_bytes=8 << 20),
    )(planes)


def exchanged(blocks, group):
    rows = blocks.shape[1]
    spare = -rows % group
    if spare:
        blocks = jnp.concatenate([blocks, jnp.zeros((DEV, spare, C), blocks.dtype)], axis=1)
    blocks = blocks.reshape(DEV, -1, group, C)
    moved = lax.all_to_all(blocks, ROW, split_axis=0, concat_axis=0, tiled=True)
    return moved.reshape(DEV, -1, C)[:, :rows]


def swapped(planes):
    parts = planes.reshape(-1, 8, 2, 8, C)
    return jnp.concatenate([parts[:, :, 1:], parts[:, :, :1]], axis=2).reshape(planes.shape)


def per_device(pair, out_grad, w_qkvg, w_out, w_bias, gain):
    pair = pair.reshape(2, 128, 2, C).transpose(0, 2, 1, 3)
    xn, normed, inv_std = normalize(pair, gain)
    bias = jnp.einsum("rcpd,dh->hrcp", xn, w_bias, preferred_element_type=F32).astype(BF16)
    columns = xn.reshape(4, 128, C)
    sent = jnp.concatenate(
        [
            jnp.broadcast_to(
                bias.reshape(2, 8, 128).transpose(1, 0, 2)[:, None, :, None], (8, 8, 2, 8, 128)
            ).reshape(8, 128, 128),
            columns,
            swapped(columns),
        ],
        axis=0,
    ).transpose(1, 0, 2)
    grads = out_grad.reshape(128, 2, 2, C).transpose(2, 1, 0, 3).reshape(2, N, C)
    grads = jnp.concatenate([grads, lax.ppermute(grads, "row_1", [(0, 1), (1, 0)])], axis=0)
    mine = lax.axis_index("row_1")
    w_own = lax.dynamic_index_in_dim(
        w_qkvg.reshape(C, 4, 2, W), mine, axis=2, keepdims=False
    ).reshape(C, 4 * W)
    wout_own = lax.dynamic_slice_in_dim(w_out, mine * W, W, axis=0)
    cols = exchanged(sent, 16).transpose(1, 0, 2)
    planes = attention(cols, grads, w_own, w_own.T, wout_own)
    back = exchanged(planes.transpose(1, 0, 2), 4).transpose(1, 0, 2)
    pairs = back.reshape(20, 8, 2, 8, C)
    d_bias = [jnp.sum(pairs[:8, :, m].astype(F32), axis=(1, 2)) for m in range(2)]
    d_bias = jnp.concatenate(d_bias, axis=0).reshape(H, 2, 2, 128)
    own_w = [jnp.sum(pairs[16:19, :, m].astype(F32), axis=(1, 2)) for m in range(2)]
    own_w = jnp.concatenate(
        [
            own_w[0][:2],
            own_w[1][:2],
            jnp.concatenate([own_w[0][2:, :W], own_w[1][2:, :W]], axis=1),
        ],
        axis=0,
    )
    d_att_x = back[8:12].astype(F32) + swapped(back[12:16]).astype(F32)
    d_att_x = d_att_x.reshape(2, 2, 128, C)
    d_bias_x = jnp.einsum(
        "hrcp,dh->rcpd", d_bias, w_bias.astype(F32), precision=lax.Precision.HIGHEST
    ).astype(BF16)
    d_wbias = jnp.einsum(
        "rcpd,hrcp->hd", xn.astype(F32), d_bias, precision=lax.Precision.HIGHEST
    )
    d_xn = d_att_x + d_bias_x.astype(F32)
    d_gain = jnp.sum(d_xn * normed, axis=(0, 1, 2))
    scaled = d_xn * gain
    d_pair = (
        inv_std
        * (
            scaled
            - jnp.mean(scaled, axis=-1, keepdims=True)
            - normed * jnp.mean(scaled * normed, axis=-1, keepdims=True)
        )
    ).astype(BF16)
    d_pair = d_pair.transpose(0, 2, 1, 3).reshape(2, N, C)
    own = jnp.concatenate([own_w, d_wbias, d_gain[None]], axis=0).astype(BF16)
    last = exchanged(jnp.broadcast_to(own[None], (DEV, 10, C)), 2)
    d_w, d_wout, d_wbias, d_gain = totals(last.transpose(1, 0, 2))
    return d_pair, d_w, d_wout, d_wbias.T, d_gain[0]


def solution(mesh):
    split = Mesh(
        mesh.devices.reshape(mesh.shape["crop"], 8, 2, 8), ("crop", "row_0", "row_1", "row_2")
    )
    placed = (P(CROP_ROW, None, None), P("crop", ROW, None), P(), P(), P(), P())
    return jax.shard_map(
        per_device,
        mesh=split,
        in_specs=placed,
        out_specs=(
            P(CROP_ROW, None, None),
            P("crop", None),
            P("crop", None),
            P("crop", None),
            P("crop"),
        ),
        check_vma=False,
    )
```

```python
import jax
import jax.numpy as jnp
from jax import lax
from jax.experimental import pallas as pl
from jax.experimental.pallas import tpu as pltpu
from jax.sharding import Mesh
from jax.sharding import PartitionSpec as P

DH = 32
H = 4
C = 128
N = 256
DEV = 128
W = 64
SCALE = DH ** (-0.5)
ROW = ("row_0", "row_1", "row_2")
CROP_ROW = ("crop", "row_0", "row_1", "row_2")
EPSILON = 1e-05
LOG2E = 1.4426950408889634
F32 = jnp.float32
BF16 = jnp.bfloat16


def dot(a, b, ca=1, cb=0):
    return lax.dot_general(a, b, (((ca,), (cb,)), ((), ())), preferred_element_type=F32)


def normalize(pair, gain):
    values = pair.astype(F32)
    center = jnp.mean(values, axis=-1, keepdims=True)
    spread = jnp.mean(jnp.square(values - center), axis=-1, keepdims=True)
    inv_std = lax.rsqrt(spread + EPSILON)
    normed = (values - center) * inv_std
    return ((normed * gain).astype(BF16), normed, inv_std)


def pack_kernel(pair_ref, gain_ref, wbias_ref, out_ref, cells, packed):
    cells[...] = pair_ref[...].reshape(2 * N, C).astype(F32)
    bias = []
    for plane in range(4):
        r, c = plane // 2, plane % 2
        xn, _, _ = normalize(cells[pl.ds(r * N + c, 128, stride=2), :], gain_ref[...])
        bias.append(dot(wbias_ref[...], xn, 1, 1).astype(BF16).astype(F32))
        xn = xn.astype(F32)
        packed[pl.ds(plane, 128, stride=8), :] = xn
        packed[pl.ds(4 + plane, 128, stride=8), :] = swapped(xn[None])[0]
    heads = [
        jnp.concatenate(
            [bias[plane][h : h + 1] for h in (2 * m, 2 * m + 1) for plane in range(4)], axis=0
        )
        for m in range(2)
    ]
    rows = jnp.concatenate([jnp.broadcast_to(x[None], (8, 8, C)) for x in heads], axis=0)
    rows = jnp.concatenate([rows] * 8, axis=0)
    out_ref[...] = jnp.concatenate([rows, packed[...].reshape(DEV, 8, C)], axis=1).astype(BF16)


def pack(pair, gain, w_bias):
    return pl.pallas_call(
        pack_kernel,
        out_shape=jax.ShapeDtypeStruct((DEV, 16, C), BF16),
        in_specs=vmem(3),
        out_specs=vmem(1)[0],
        scratch_shapes=[pltpu.VMEM((2 * N, C), F32), pltpu.VMEM((8 * DEV, C), F32)],
    )(pair, gain.reshape(1, C), w_bias.T)


def attention_kernel(cols_ref, grad_ref, w_ref, wt_ref, wout_ref, out_ref):
    def prepare(t):
        at = 8 + 4 * (t // 2) + t % 2
        tokens = jnp.concatenate([cols_ref[at], cols_ref[at + 2]], axis=0)
        grads = grad_ref[t]
        proj = dot(tokens, w_ref[:, : 3 * W]).astype(BF16)
        proj_t = dot(wt_ref[...], tokens, 1, 1)
        gate_t = jax.nn.sigmoid(proj_t[3 * W :])
        d_mixed_t = dot(wout_ref[...], grads, 1, 1)
        d_att_t = (d_mixed_t * gate_t).astype(BF16)
        return dict(
            tokens=tokens,
            grads=grads,
            q=proj[:, :W],
            k=proj[:, W : 2 * W],
            v=proj[:, 2 * W :],
            q_t=proj_t[:W].astype(BF16),
            k_t=proj_t[W : 2 * W].astype(BF16),
            v_t=proj_t[2 * W : 3 * W].astype(BF16),
            gate_t=gate_t,
            d_mixed_t=d_mixed_t,
            d_att_t=d_att_t,
            d_att=d_att_t.T,
            att_h=[],
            dq_h=[],
            d_k=None,
            d_v=None,
        )

    lane = lax.broadcasted_iota(jnp.int32, (N, W), 1) // DH
    zero = jnp.zeros((N, W), BF16)

    def raw(col, h):
        rows = slice(h * DH, (h + 1) * DH)
        s = dot(col["k"][:, rows], col["q_t"][rows])
        d_probs = dot(col["v"][:, rows], col["d_att_t"][rows])
        return s, d_probs

    def head(col, h, bias, s, d_probs):
        own = lane == h
        rows = slice(h * DH, (h + 1) * DH)
        s = s * (SCALE * LOG2E) + bias
        e = jnp.exp2(s - jnp.max(s, axis=0, keepdims=True))
        probs = e * (1.0 / jnp.sum(e, axis=0, keepdims=True))
        probs_b = probs.astype(BF16)
        att_h = dot(col["v_t"][rows], probs_b)
        delta = jnp.sum(col["d_att_t"][rows].astype(F32) * att_h, axis=0, keepdims=True)
        d_s = probs * (d_probs - delta)
        d_sb = d_s.astype(BF16)
        col["att_h"].append(att_h)
        col["dq_h"].append(dot(col["k_t"][rows], d_sb))
        dk_h = dot(d_sb, jnp.where(own, col["q"], zero))
        dv_h = dot(probs_b, jnp.where(own, col["d_att"], zero))
        col["d_k"] = dk_h if h == 0 else col["d_k"] + dk_h
        col["d_v"] = dv_h if h == 0 else col["d_v"] + dv_h
        return d_s

    def finish(col):
        att_t = jnp.concatenate(col["att_h"], axis=0)
        gate_t = col["gate_t"]
        mixed_t = (gate_t * att_t).astype(BF16)
        d_gate_t = (col["d_mixed_t"] * att_t * gate_t * (1.0 - gate_t)).astype(BF16)
        d_q_t = (jnp.concatenate(col["dq_h"], axis=0) * SCALE).astype(BF16)
        d_proj = jnp.concatenate(
            [d_q_t.T, (col["d_k"] * SCALE).astype(BF16), col["d_v"].astype(BF16), d_gate_t.T],
            axis=1,
        )
        d_tokens = dot(d_proj, wt_ref[...]).astype(BF16)
        return dot(col["tokens"], d_proj, 0, 0), dot(mixed_t, col["grads"]), d_tokens

    def bias_of(h):
        return (
            jnp.concatenate(
                [
                    jnp.concatenate([cols_ref[4 * h + 2 * r], cols_ref[4 * h + 2 * r + 1]], axis=1)
                    for r in range(2)
                ],
                axis=0,
            ).astype(F32)
            * LOG2E
        )

    cols = [prepare(t) for t in range(4)]
    order = [(h, t) for h in range(2) for t in range(4)]
    ahead = raw(cols[0], 0)
    for step, (h, t) in enumerate(order):
        s, d_probs = ahead
        if step + 1 < len(order):
            ahead = raw(cols[order[step + 1][1]], order[step + 1][0])
        if t == 0:
            bias, total = bias_of(h), 0.0
        total = total + head(cols[t], h, bias, s, d_probs)
        if t == 3:
            total = total.astype(BF16)
            for r in range(2):
                for half in range(2):
                    out_ref[4 * h + 2 * r + half] = total[
                        r * 128 : (r + 1) * 128, half * 128 : (half + 1) * 128
                    ]
    d_w, d_wout = 0.0, 0.0
    for t in range(4):
        part_w, part_wout, d_tokens = finish(cols[t])
        d_w, d_wout = d_w + part_w, d_wout + part_wout
        at = 8 + 4 * (t // 2) + t % 2
        out_ref[at] = d_tokens[:128]
        out_ref[at + 2] = d_tokens[128:]
    d_w, d_wout = d_w.astype(BF16), d_wout.astype(BF16)
    for block in range(2):
        out_ref[16 + block] = d_w[:, block * C : (block + 1) * C]
    out_ref[18] = jnp.concatenate(
        [
            jnp.concatenate([d_wout[:, :W], d_wout[:, W:]], axis=0),
            jnp.zeros((DEV, W), BF16),
        ],
        axis=1,
    )
    out_ref[19] = jnp.zeros((DEV, C), BF16)


def vmem(count):
    return [pl.BlockSpec(memory_space=pltpu.VMEM)] * count


def attention(cols, grads, w, w_t, w_out):
    return pl.pallas_call(
        attention_kernel,
        out_shape=jax.ShapeDtypeStruct((20, DEV, C), BF16),
        in_specs=vmem(5),
        out_specs=vmem(1)[0],
        compiler_params=pltpu.CompilerParams(
            vmem_limit_bytes=24 << 20
        ),
        cost_estimate=pl.CostEstimate(
            flops=900_000_000, bytes_accessed=3_000_000, transcendentals=600_000
        ),
    )(cols, grads, w, w_t, w_out)


def totals_kernel(planes_ref, w_ref, wout_ref, wbias_ref, gain_ref):
    scale = 1.0 / N
    for block in range(4):
        at = slice((block % 2) * W, (block % 2 + 1) * W)
        w_ref[:, block * C : (block + 1) * C] = (
            jnp.concatenate(
                [planes_ref[2 * pair + block // 2].astype(F32)[:, at] for pair in range(2)], axis=1
            )
            * scale
        )
    shares = planes_ref[4].astype(F32) * scale
    for pair in range(2):
        own = shares[:, pair * W : (pair + 1) * W]
        wout_ref[pair * W : (pair + 1) * W] = jnp.concatenate([own[:W], own[W:]], axis=1)
    for h in range(H):
        wbias_ref[h : h + 1] = (
            jnp.sum(planes_ref[5 + h].astype(F32), axis=0, keepdims=True) * scale
        )
    gain_ref[...] = jnp.sum(planes_ref[9].astype(F32), axis=0, keepdims=True) * scale


def totals(planes):
    return pl.pallas_call(
        totals_kernel,
        out_shape=(
            jax.ShapeDtypeStruct((C, 4 * C), F32),
            jax.ShapeDtypeStruct((C, C), F32),
            jax.ShapeDtypeStruct((H, C), F32),
            jax.ShapeDtypeStruct((1, C), F32),
        ),
        in_specs=vmem(1),
        out_specs=tuple(vmem(4)),
        compiler_params=pltpu.CompilerParams(vmem_limit_bytes=8 << 20),
    )(planes)


def exchanged(blocks, group):
    rows = blocks.shape[1]
    spare = -rows % group
    if spare:
        blocks = jnp.concatenate([blocks, jnp.zeros((DEV, spare, C), blocks.dtype)], axis=1)
    blocks = blocks.reshape(DEV, -1, group, C)
    moved = lax.all_to_all(blocks, ROW, split_axis=0, concat_axis=0, tiled=True)
    return moved.reshape(DEV, -1, C)[:, :rows]


def swapped(planes):
    parts = planes.reshape(-1, 8, 2, 8, C)
    return jnp.concatenate([parts[:, :, 1:], parts[:, :, :1]], axis=2).reshape(planes.shape)


def per_device(pair, out_grad, w_qkvg, w_out, w_bias, gain):
    sent = pack(pair, gain, w_bias)
    pair = pair.reshape(2, 128, 2, C).transpose(0, 2, 1, 3)
    xn, normed, inv_std = normalize(pair, gain)
    grads = out_grad.reshape(128, 2, 2, C).transpose(2, 1, 0, 3).reshape(2, N, C)
    grads = jnp.concatenate([grads, lax.ppermute(grads, "row_1", [(0, 1), (1, 0)])], axis=0)
    mine = lax.axis_index("row_1")
    w_own = lax.dynamic_index_in_dim(
        w_qkvg.reshape(C, 4, 2, W), mine, axis=2, keepdims=False
    ).reshape(C, 4 * W)
    wout_own = lax.dynamic_slice_in_dim(w_out, mine * W, W, axis=0)
    cols = exchanged(sent, 16).transpose(1, 0, 2)
    planes = attention(cols, grads, w_own, w_own.T, wout_own)
    back = exchanged(planes.transpose(1, 0, 2), 4).transpose(1, 0, 2)
    pairs = back.reshape(20, 8, 2, 8, C)
    d_bias = [jnp.sum(pairs[:8, :, m].astype(F32), axis=(1, 2)) for m in range(2)]
    d_bias = jnp.concatenate(d_bias, axis=0).reshape(H, 2, 2, 128)
    own_w = [jnp.sum(pairs[16:19, :, m].astype(F32), axis=(1, 2)) for m in range(2)]
    own_w = jnp.concatenate(
        [
            own_w[0][:2],
            own_w[1][:2],
            jnp.concatenate([own_w[0][2:, :W], own_w[1][2:, :W]], axis=1),
        ],
        axis=0,
    )
    d_att_x = back[8:12].astype(F32) + swapped(back[12:16]).astype(F32)
    d_att_x = d_att_x.reshape(2, 2, 128, C)
    d_bias_x = jnp.einsum(
        "hrcp,dh->rcpd", d_bias, w_bias.astype(F32), precision=lax.Precision.HIGHEST
    ).astype(BF16)
    d_wbias = jnp.einsum(
        "rcpd,hrcp->hd", xn.astype(F32), d_bias, precision=lax.Precision.HIGHEST
    )
    d_xn = d_att_x + d_bias_x.astype(F32)
    d_gain = jnp.sum(d_xn * normed, axis=(0, 1, 2))
    scaled = d_xn * gain
    d_pair = (
        inv_std
        * (
            scaled
            - jnp.mean(scaled, axis=-1, keepdims=True)
            - normed * jnp.mean(scaled * normed, axis=-1, keepdims=True)
        )
    ).astype(BF16)
    d_pair = d_pair.transpose(0, 2, 1, 3).reshape(2, N, C)
    own = jnp.concatenate([own_w, d_wbias, d_gain[None]], axis=0).astype(BF16)
    last = exchanged(jnp.broadcast_to(own[None], (DEV, 10, C)), 2)
    d_w, d_wout, d_wbias, d_gain = totals(last.transpose(1, 0, 2))
    return d_pair, d_w, d_wout, d_wbias.T, d_gain[0]


def solution(mesh):
    split = Mesh(
        mesh.devices.reshape(mesh.shape["crop"], 8, 2, 8), ("crop", "row_0", "row_1", "row_2")
    )
    placed = (P(CROP_ROW, None, None), P("crop", ROW, None), P(), P(), P(), P())
    return jax.shard_map(
        per_device,
        mesh=split,
        in_specs=placed,
        out_specs=(
            P(CROP_ROW, None, None),
            P("crop", None),
            P("crop", None),
            P("crop", None),
            P("crop"),
        ),
        check_vma=False,
    )
```

```python
import jax
import jax.numpy as jnp
from jax import lax
from jax.experimental import pallas as pl
from jax.experimental.pallas import tpu as pltpu
from jax.sharding import Mesh
from jax.sharding import PartitionSpec as P

DH = 32
H = 4
C = 128
N = 256
DEV = 128
W = 64
SCALE = DH ** (-0.5)
ROW = ("row_0", "row_1", "row_2")
CROP_ROW = ("crop", "row_0", "row_1", "row_2")
EPSILON = 1e-05
LOG2E = 1.4426950408889634
F32 = jnp.float32
BF16 = jnp.bfloat16


def dot(a, b, ca=1, cb=0):
    return lax.dot_general(a, b, (((ca,), (cb,)), ((), ())), preferred_element_type=F32)


def normalize(pair, gain):
    values = pair.astype(F32)
    center = jnp.mean(values, axis=-1, keepdims=True)
    spread = jnp.mean(jnp.square(values - center), axis=-1, keepdims=True)
    inv_std = lax.rsqrt(spread + EPSILON)
    normed = (values - center) * inv_std
    return ((normed * gain).astype(BF16), normed, inv_std)


def pack_kernel(pair_ref, gain_ref, wbias_ref, out_ref, cells, packed):
    cells[...] = pair_ref[...].reshape(2 * N, C).astype(F32)
    bias = []
    for plane in range(4):
        r, c = plane // 2, plane % 2
        xn, _, _ = normalize(cells[pl.ds(r * N + c, 128, stride=2), :], gain_ref[...])
        bias.append(dot(wbias_ref[...], xn, 1, 1).astype(BF16).astype(F32))
        xn = xn.astype(F32)
        packed[pl.ds(plane, 128, stride=8), :] = xn
        packed[pl.ds(4 + plane, 128, stride=8), :] = swapped(xn[None])[0]
    heads = [
        jnp.concatenate(
            [bias[plane][h : h + 1] for h in (2 * m, 2 * m + 1) for plane in range(4)], axis=0
        )
        for m in range(2)
    ]
    rows = jnp.concatenate([jnp.broadcast_to(x[None], (8, 8, C)) for x in heads], axis=0)
    rows = jnp.concatenate([rows] * 8, axis=0)
    out_ref[...] = jnp.concatenate([rows, packed[...].reshape(DEV, 8, C)], axis=1).astype(BF16)


def pack(pair, gain, w_bias):
    return pl.pallas_call(
        pack_kernel,
        out_shape=jax.ShapeDtypeStruct((DEV, 16, C), BF16),
        in_specs=vmem(3),
        out_specs=vmem(1)[0],
        scratch_shapes=[pltpu.VMEM((2 * N, C), F32), pltpu.VMEM((8 * DEV, C), F32)],
    )(pair, gain.reshape(1, C), w_bias.T)


def attention_kernel(cols_ref, grad_ref, w_ref, wt_ref, wout_ref, out_ref):
    def prepare(t):
        at = 8 + 4 * (t // 2) + t % 2
        tokens = jnp.concatenate([cols_ref[at], cols_ref[at + 2]], axis=0)
        grads = grad_ref[t]
        proj = dot(tokens, w_ref[:, : 3 * W]).astype(BF16)
        proj_t = dot(wt_ref[...], tokens, 1, 1)
        gate_t = jax.nn.sigmoid(proj_t[3 * W :])
        d_mixed_t = dot(wout_ref[...], grads, 1, 1)
        d_att_t = (d_mixed_t * gate_t).astype(BF16)
        return dict(
            tokens=tokens,
            grads=grads,
            q=proj[:, :W],
            k=proj[:, W : 2 * W],
            v=proj[:, 2 * W :],
            q_t=proj_t[:W].astype(BF16),
            k_t=proj_t[W : 2 * W].astype(BF16),
            v_t=proj_t[2 * W : 3 * W].astype(BF16),
            gate_t=gate_t,
            d_mixed_t=d_mixed_t,
            d_att_t=d_att_t,
            d_att=d_att_t.T,
            att_h=[],
            dq_h=[],
            d_k=None,
            d_v=None,
        )

    lane = lax.broadcasted_iota(jnp.int32, (N, W), 1) // DH
    zero = jnp.zeros((N, W), BF16)

    def raw(col, h):
        rows = slice(h * DH, (h + 1) * DH)
        s = dot(col["k"][:, rows], col["q_t"][rows])
        d_probs = dot(col["v"][:, rows], col["d_att_t"][rows])
        return s, d_probs

    def head(col, h, bias, s, d_probs):
        own = lane == h
        rows = slice(h * DH, (h + 1) * DH)
        s = s * (SCALE * LOG2E) + bias
        e = jnp.exp2(s - jnp.max(s, axis=0, keepdims=True))
        probs = e * (1.0 / jnp.sum(e, axis=0, keepdims=True))
        probs_b = probs.astype(BF16)
        att_h = dot(col["v_t"][rows], probs_b)
        delta = jnp.sum(col["d_att_t"][rows].astype(F32) * att_h, axis=0, keepdims=True)
        d_s = probs * (d_probs - delta)
        d_sb = d_s.astype(BF16)
        col["att_h"].append(att_h)
        col["dq_h"].append(dot(col["k_t"][rows], d_sb))
        dk_h = dot(d_sb, jnp.where(own, col["q"], zero))
        dv_h = dot(probs_b, jnp.where(own, col["d_att"], zero))
        col["d_k"] = dk_h if h == 0 else col["d_k"] + dk_h
        col["d_v"] = dv_h if h == 0 else col["d_v"] + dv_h
        return d_s

    def finish(col):
        att_t = jnp.concatenate(col["att_h"], axis=0)
        gate_t = col["gate_t"]
        mixed_t = (gate_t * att_t).astype(BF16)
        d_gate_t = (col["d_mixed_t"] * att_t * gate_t * (1.0 - gate_t)).astype(BF16)
        d_q_t = (jnp.concatenate(col["dq_h"], axis=0) * SCALE).astype(BF16)
        d_proj = jnp.concatenate(
            [d_q_t.T, (col["d_k"] * SCALE).astype(BF16), col["d_v"].astype(BF16), d_gate_t.T],
            axis=1,
        )
        d_tokens = dot(d_proj, wt_ref[...]).astype(BF16)
        return dot(col["tokens"], d_proj, 0, 0), dot(mixed_t, col["grads"]), d_tokens

    def bias_of(h):
        return (
            jnp.concatenate(
                [
                    jnp.concatenate([cols_ref[4 * h + 2 * r], cols_ref[4 * h + 2 * r + 1]], axis=1)
                    for r in range(2)
                ],
                axis=0,
            ).astype(F32)
            * LOG2E
        )

    cols = [prepare(t) for t in range(4)]
    order = [(h, t) for h in range(2) for t in range(4)]
    ahead = raw(cols[0], 0)
    for step, (h, t) in enumerate(order):
        s, d_probs = ahead
        if step + 1 < len(order):
            ahead = raw(cols[order[step + 1][1]], order[step + 1][0])
        if t == 0:
            bias, total = bias_of(h), 0.0
        total = total + head(cols[t], h, bias, s, d_probs)
        if t == 3:
            total = total.astype(BF16)
            for r in range(2):
                for half in range(2):
                    out_ref[4 * h + 2 * r + half] = total[
                        r * 128 : (r + 1) * 128, half * 128 : (half + 1) * 128
                    ]
    d_w, d_wout = 0.0, 0.0
    for t in range(4):
        part_w, part_wout, d_tokens = finish(cols[t])
        d_w, d_wout = d_w + part_w, d_wout + part_wout
        at = 8 + 4 * (t // 2) + t % 2
        out_ref[at] = d_tokens[:128]
        out_ref[at + 2] = d_tokens[128:]
    d_w, d_wout = d_w.astype(BF16), d_wout.astype(BF16)
    for block in range(2):
        out_ref[16 + block] = d_w[:, block * C : (block + 1) * C]
    out_ref[18] = jnp.concatenate(
        [
            jnp.concatenate([d_wout[:, :W], d_wout[:, W:]], axis=0),
            jnp.zeros((DEV, W), BF16),
        ],
        axis=1,
    )
    out_ref[19] = jnp.zeros((DEV, C), BF16)


def vmem(count):
    return [pl.BlockSpec(memory_space=pltpu.VMEM)] * count


def attention(cols, grads, w, w_t, w_out):
    return pl.pallas_call(
        attention_kernel,
        out_shape=jax.ShapeDtypeStruct((20, DEV, C), BF16),
        in_specs=vmem(5),
        out_specs=vmem(1)[0],
        compiler_params=pltpu.CompilerParams(
            vmem_limit_bytes=24 << 20
        ),
        cost_estimate=pl.CostEstimate(
            flops=900_000_000, bytes_accessed=3_000_000, transcendentals=600_000
        ),
    )(cols, grads, w, w_t, w_out)


def middle_kernel(back_ref, xn_ref, normed_ref, wbias_ref, out_ref, d_xn_ref):
    def sums(row):
        parts = back_ref[row].astype(F32).reshape(8, 2, 8, C)
        return [jnp.sum(jnp.sum(parts[:, m], axis=0), axis=0, keepdims=True) for m in range(2)]

    d_bias = [sums(row) for row in range(8)]
    weights = [sums(row) for row in range(16, 19)]
    w_three = jnp.concatenate([wbias_ref[...]] * 3, axis=0).astype(BF16)
    d_wbias, d_gain = 0.0, 0.0
    for plane in range(4):
        owned = jnp.concatenate([d_bias[4 * (h % 2) + plane][h // 2] for h in range(H)], axis=0)
        terms = [owned.astype(BF16)]
        left = owned - terms[0].astype(F32)
        terms.append(left.astype(BF16))
        terms.append((left - terms[1].astype(F32)).astype(BF16))
        three = jnp.concatenate(terms, axis=0)
        d_bias_x = dot(three, w_three, 0, 0).astype(BF16).astype(F32)
        d_att_x = back_ref[8 + plane].astype(F32) + swapped(back_ref[12 + plane].astype(F32)[None])[0]
        d_xn = d_att_x + d_bias_x
        d_xn_ref[plane] = d_xn
        d_gain = d_gain + jnp.sum(d_xn * normed_ref[plane], axis=0, keepdims=True)
        parts = dot(three, xn_ref[plane])
        d_wbias = d_wbias + (parts[:H] + parts[H : 2 * H] + parts[2 * H :])
    rows = [
        weights[0][0],
        weights[1][0],
        weights[0][1],
        weights[1][1],
        jnp.concatenate([weights[2][0][:, :W], weights[2][1][:, :W]], axis=1),
    ]
    rows = jnp.concatenate(rows + [d_wbias, d_gain], axis=0)
    for at in range(5):
        out_ref[:, at] = jnp.broadcast_to(
            rows[2 * at : 2 * at + 2].astype(BF16)[None], (DEV, 2, C)
        )


def middle(back, xn, normed, heads_bias):
    return pl.pallas_call(
        middle_kernel,
        out_shape=(
            jax.ShapeDtypeStruct((DEV, 5, 2, C), BF16),
            jax.ShapeDtypeStruct((4, DEV, C), F32),
        ),
        in_specs=vmem(4),
        out_specs=tuple(vmem(2)),
        compiler_params=pltpu.CompilerParams(vmem_limit_bytes=16 << 20),
    )(back, xn, normed, heads_bias)


def totals_kernel(planes_ref, w_ref, wout_ref, wbias_ref, gain_ref):
    scale = 1.0 / N
    for block in range(4):
        at = slice((block % 2) * W, (block % 2 + 1) * W)
        w_ref[:, block * C : (block + 1) * C] = (
            jnp.concatenate(
                [planes_ref[2 * pair + block // 2].astype(F32)[:, at] for pair in range(2)], axis=1
            )
            * scale
        )
    shares = planes_ref[4].astype(F32) * scale
    for pair in range(2):
        own = shares[:, pair * W : (pair + 1) * W]
        wout_ref[pair * W : (pair + 1) * W] = jnp.concatenate([own[:W], own[W:]], axis=1)
    for h in range(H):
        wbias_ref[h : h + 1] = (
            jnp.sum(planes_ref[5 + h].astype(F32), axis=0, keepdims=True) * scale
        )
    gain_ref[...] = jnp.sum(planes_ref[9].astype(F32), axis=0, keepdims=True) * scale


def totals(planes):
    return pl.pallas_call(
        totals_kernel,
        out_shape=(
            jax.ShapeDtypeStruct((C, 4 * C), F32),
            jax.ShapeDtypeStruct((C, C), F32),
            jax.ShapeDtypeStruct((H, C), F32),
            jax.ShapeDtypeStruct((1, C), F32),
        ),
        in_specs=vmem(1),
        out_specs=tuple(vmem(4)),
        compiler_params=pltpu.CompilerParams(vmem_limit_bytes=8 << 20),
    )(planes)


def exchanged(blocks, group):
    rows = blocks.shape[1]
    spare = -rows % group
    if spare:
        blocks = jnp.concatenate([blocks, jnp.zeros((DEV, spare, C), blocks.dtype)], axis=1)
    blocks = blocks.reshape(DEV, -1, group, C)
    moved = lax.all_to_all(blocks, ROW, split_axis=0, concat_axis=0, tiled=True)
    return moved.reshape(DEV, -1, C)[:, :rows]


def swapped(planes):
    parts = planes.reshape(-1, 8, 2, 8, C)
    return jnp.concatenate([parts[:, :, 1:], parts[:, :, :1]], axis=2).reshape(planes.shape)


def per_device(pair, out_grad, w_qkvg, w_out, w_bias, gain):
    sent = pack(pair, gain, w_bias)
    sent, out_grad = lax.optimization_barrier((sent, out_grad))
    pair = pair.reshape(2, 128, 2, C).transpose(0, 2, 1, 3)
    xn, normed, inv_std = normalize(pair, gain)
    grads = out_grad.reshape(128, 2, 2, C).transpose(2, 1, 0, 3).reshape(2, N, C)
    grads = jnp.concatenate([grads, lax.ppermute(grads, "row_1", [(0, 1), (1, 0)])], axis=0)
    grads, xn, normed, inv_std, gain, heads_bias = lax.optimization_barrier(
        (grads, xn, normed, inv_std, gain, w_bias.T.astype(F32))
    )
    mine = lax.axis_index("row_1")
    w_own = lax.dynamic_index_in_dim(
        w_qkvg.reshape(C, 4, 2, W), mine, axis=2, keepdims=False
    ).reshape(C, 4 * W)
    wout_own = lax.dynamic_slice_in_dim(w_out, mine * W, W, axis=0)
    cols = exchanged(sent, 16).transpose(1, 0, 2)
    planes = attention(cols, grads, w_own, w_own.T, wout_own)
    back = exchanged(planes.transpose(1, 0, 2), 4).transpose(1, 0, 2)
    last, d_xn = middle(back, xn.reshape(4, 128, C), normed.reshape(4, 128, C), heads_bias)
    d_xn = d_xn.reshape(2, 2, 128, C)
    scaled = d_xn * gain
    d_pair = (
        inv_std
        * (
            scaled
            - jnp.mean(scaled, axis=-1, keepdims=True)
            - normed * jnp.mean(scaled * normed, axis=-1, keepdims=True)
        )
    ).astype(BF16)
    d_pair = d_pair.transpose(0, 2, 1, 3).reshape(2, N, C)
    last = lax.all_to_all(last, ROW, split_axis=0, concat_axis=0, tiled=True).reshape(DEV, 10, C)
    d_w, d_wout, d_wbias, d_gain = totals(last.transpose(1, 0, 2))
    return d_pair, d_w, d_wout, d_wbias.T, d_gain[0]


def solution(mesh):
    split = Mesh(
        mesh.devices.reshape(mesh.shape["crop"], 8, 2, 8), ("crop", "row_0", "row_1", "row_2")
    )
    placed = (P(CROP_ROW, None, None), P("crop", ROW, None), P(), P(), P(), P())
    return jax.shard_map(
        per_device,
        mesh=split,
        in_specs=placed,
        out_specs=(
            P(CROP_ROW, None, None),
            P("crop", None),
            P("crop", None),
            P("crop", None),
            P("crop"),
        ),
        check_vma=False,
    )
```

```python
import jax
import jax.numpy as jnp
from jax import lax
from jax.experimental import pallas as pl
from jax.experimental.pallas import tpu as pltpu
from jax.sharding import Mesh
from jax.sharding import PartitionSpec as P

DH = 32
H = 4
C = 128
N = 256
DEV = 128
W = 64
SCALE = DH ** (-0.5)
ROW = ("row_0", "row_1", "row_2")
CROP_ROW = ("crop", "row_0", "row_1", "row_2")
EPSILON = 1e-05
LOG2E = 1.4426950408889634
F32 = jnp.float32
BF16 = jnp.bfloat16


def dot(a, b, ca=1, cb=0):
    return lax.dot_general(a, b, (((ca,), (cb,)), ((), ())), preferred_element_type=F32)


def normalize(pair, gain):
    values = pair.astype(F32)
    center = jnp.mean(values, axis=-1, keepdims=True)
    spread = jnp.mean(jnp.square(values - center), axis=-1, keepdims=True)
    inv_std = lax.rsqrt(spread + EPSILON)
    normed = (values - center) * inv_std
    return ((normed * gain).astype(BF16), normed, inv_std)


def doubled(plane, m):
    own = plane.reshape(8, 2, 8, C)[:, m : m + 1]
    return jnp.concatenate([own, own], axis=1).reshape(128, C)


def member(rows, m):
    return rows.reshape(8, 2, 8, -1)[:, m].reshape(64, -1)


def pack_kernel(pair_ref, gain_ref, wbias_ref, out_ref, cells, packed):
    cells[...] = pair_ref[...].reshape(2 * N, C).astype(F32)
    bias = []
    for plane in range(4):
        r, c = plane // 2, plane % 2
        xn, _, _ = normalize(cells[pl.ds(r * N + c, 128, stride=2), :], gain_ref[...])
        bias.append(dot(wbias_ref[...], xn, 1, 1).astype(BF16).astype(F32))
        xn = xn.astype(F32)
        for m in range(2):
            packed[pl.ds(4 * m + plane, 128, stride=8), :] = doubled(xn, m)
    heads = [
        jnp.concatenate(
            [bias[plane][h : h + 1] for h in (2 * m, 2 * m + 1) for plane in range(4)], axis=0
        )
        for m in range(2)
    ]
    rows = jnp.concatenate([jnp.broadcast_to(x[None], (8, 8, C)) for x in heads], axis=0)
    rows = jnp.concatenate([rows] * 8, axis=0)
    out_ref[...] = jnp.concatenate([rows, packed[...].reshape(DEV, 8, C)], axis=1).astype(BF16)


def pack(pair, gain, w_bias):
    return pl.pallas_call(
        pack_kernel,
        out_shape=jax.ShapeDtypeStruct((DEV, 16, C), BF16),
        in_specs=vmem(3),
        out_specs=vmem(1)[0],
        scratch_shapes=[pltpu.VMEM((2 * N, C), F32), pltpu.VMEM((8 * DEV, C), F32)],
    )(pair, gain.reshape(1, C), w_bias.T)


def attention_kernel(cols_ref, grad_ref, w_ref, wt_ref, wout_ref, out_ref):
    def prepare(t):
        at = 8 + 4 * (t // 2) + t % 2
        tokens = jnp.concatenate([cols_ref[at], cols_ref[at + 2]], axis=0)
        grads = grad_ref[t]
        proj = dot(tokens, w_ref[:, : 3 * W]).astype(BF16)
        proj_t = dot(wt_ref[...], tokens, 1, 1)
        gate_t = jax.nn.sigmoid(proj_t[3 * W :])
        d_mixed_t = dot(wout_ref[...], grads, 1, 1)
        d_att_t = (d_mixed_t * gate_t).astype(BF16)
        return dict(
            tokens=tokens,
            grads=grads,
            q=proj[:, :W],
            k=proj[:, W : 2 * W],
            v=proj[:, 2 * W :],
            q_t=proj_t[:W].astype(BF16),
            k_t=proj_t[W : 2 * W].astype(BF16),
            v_t=proj_t[2 * W : 3 * W].astype(BF16),
            gate_t=gate_t,
            d_mixed_t=d_mixed_t,
            d_att_t=d_att_t,
            d_att=d_att_t.T,
            att_h=[],
            dq_h=[],
            d_k=None,
            d_v=None,
        )

    lane = lax.broadcasted_iota(jnp.int32, (N, W), 1) // DH
    zero = jnp.zeros((N, W), BF16)

    def raw(col, h):
        rows = slice(h * DH, (h + 1) * DH)
        s = dot(col["k"][:, rows], col["q_t"][rows])
        d_probs = dot(col["v"][:, rows], col["d_att_t"][rows])
        return s, d_probs

    def head(col, h, bias, s, d_probs):
        own = lane == h
        rows = slice(h * DH, (h + 1) * DH)
        s = s * (SCALE * LOG2E) + bias
        e = jnp.exp2(s - jnp.max(s, axis=0, keepdims=True))
        probs = e * (1.0 / jnp.sum(e, axis=0, keepdims=True))
        probs_b = probs.astype(BF16)
        att_h = dot(col["v_t"][rows], probs_b)
        delta = jnp.sum(col["d_att_t"][rows].astype(F32) * att_h, axis=0, keepdims=True)
        d_s = probs * (d_probs - delta)
        d_sb = d_s.astype(BF16)
        col["att_h"].append(att_h)
        col["dq_h"].append(dot(col["k_t"][rows], d_sb))
        dk_h = dot(d_sb, jnp.where(own, col["q"], zero))
        dv_h = dot(probs_b, jnp.where(own, col["d_att"], zero))
        col["d_k"] = dk_h if h == 0 else col["d_k"] + dk_h
        col["d_v"] = dv_h if h == 0 else col["d_v"] + dv_h
        return d_s

    def finish(col):
        att_t = jnp.concatenate(col["att_h"], axis=0)
        gate_t = col["gate_t"]
        mixed_t = (gate_t * att_t).astype(BF16)
        d_gate_t = (col["d_mixed_t"] * att_t * gate_t * (1.0 - gate_t)).astype(BF16)
        d_q_t = (jnp.concatenate(col["dq_h"], axis=0) * SCALE).astype(BF16)
        d_proj = jnp.concatenate(
            [d_q_t.T, (col["d_k"] * SCALE).astype(BF16), col["d_v"].astype(BF16), d_gate_t.T],
            axis=1,
        )
        d_tokens = dot(d_proj, wt_ref[...])
        return dot(col["tokens"], d_proj, 0, 0), dot(mixed_t, col["grads"]), d_tokens

    def bias_of(h):
        return (
            jnp.concatenate(
                [
                    jnp.concatenate([cols_ref[4 * h + 2 * r], cols_ref[4 * h + 2 * r + 1]], axis=1)
                    for r in range(2)
                ],
                axis=0,
            ).astype(F32)
            * LOG2E
        )

    cols = [prepare(t) for t in range(4)]
    order = [(h, t) for h in range(2) for t in range(4)]
    ahead = raw(cols[0], 0)
    for step, (h, t) in enumerate(order):
        s, d_probs = ahead
        if step + 1 < len(order):
            ahead = raw(cols[order[step + 1][1]], order[step + 1][0])
        if t == 0:
            bias, total = bias_of(h), 0.0
        total = total + head(cols[t], h, bias, s, d_probs)
        if t == 3:
            for r in range(2):
                for m in range(2):
                    part = member(total[r * 128 : (r + 1) * 128], m).astype(BF16)
                    for half in range(2):
                        out_ref[8 * h + 4 * m + 2 * r + half] = part[
                            :, half * 128 : (half + 1) * 128
                        ]
    d_w, d_wout = 0.0, 0.0
    for t in range(4):
        part_w, part_wout, d_tokens = finish(cols[t])
        d_w, d_wout = d_w + part_w, d_wout + part_wout
        for r in range(2):
            for m in range(2):
                at = 16 + 8 * m + 4 * (t // 2) + 2 * r + t % 2
                out_ref[at] = member(d_tokens[r * 128 : (r + 1) * 128], m).astype(BF16)
    d_w = d_w.astype(BF16)
    for u in range(2):
        for block in range(2):
            out_ref[32 + 2 * u + block] = d_w[
                u * 64 : (u + 1) * 64, block * C : (block + 1) * C
            ]
    out_ref[36] = d_wout.astype(BF16)
    out_ref[37] = jnp.zeros((64, C), BF16)


def vmem(count):
    return [pl.BlockSpec(memory_space=pltpu.VMEM)] * count


def attention(cols, grads, w, w_t, w_out):
    return pl.pallas_call(
        attention_kernel,
        out_shape=jax.ShapeDtypeStruct((38, 64, C), BF16),
        in_specs=vmem(5),
        out_specs=vmem(1)[0],
        compiler_params=pltpu.CompilerParams(
            vmem_limit_bytes=24 << 20
        ),
        cost_estimate=pl.CostEstimate(
            flops=900_000_000, bytes_accessed=3_000_000, transcendentals=600_000
        ),
    )(cols, grads, w, w_t, w_out)


def middle_kernel(back_ref, xn_ref, normed_ref, wbias_ref, out_ref, d_xn_ref):
    def sums(row):
        return jnp.sum(back_ref[row].astype(F32), axis=0, keepdims=True)

    w_three = jnp.concatenate([wbias_ref[...]] * 3, axis=0).astype(BF16)
    d_wbias, d_gain = 0.0, 0.0
    for plane in range(8):
        m, cell = plane // 4, plane % 4
        owned = jnp.concatenate([sums(plane), sums(8 + plane)], axis=0)
        terms = [owned.astype(BF16)]
        left = owned - terms[0].astype(F32)
        terms.append(left.astype(BF16))
        terms.append((left - terms[1].astype(F32)).astype(BF16))
        three = jnp.concatenate(terms, axis=0)
        d_bias_x = dot(three, w_three, 0, 0)
        at = 16 + 8 * m + cell
        d_att_x = jnp.concatenate(
            [back_ref[at + 4 * j].astype(F32).reshape(8, 1, 8, C) for j in range(2)], axis=1
        )
        d_xn = d_att_x.reshape(128, C) + d_bias_x
        d_xn_ref[plane] = d_xn
        d_gain = d_gain + jnp.sum(d_xn * normed_ref[plane], axis=0, keepdims=True)
        parts = dot(three, xn_ref[plane])
        d_wbias = d_wbias + (parts[:2] + parts[2:4] + parts[4:])
    rows = jnp.concatenate([sums(row) for row in range(32, 37)] + [d_wbias, d_gain], axis=0)
    out_ref[...] = jnp.broadcast_to(rows[None], (DEV, 8, C)).astype(BF16)


def middle(back, xn, normed, heads_bias):
    return pl.pallas_call(
        middle_kernel,
        out_shape=(
            jax.ShapeDtypeStruct((DEV, 8, C), BF16),
            jax.ShapeDtypeStruct((8, DEV, C), F32),
        ),
        in_specs=vmem(4),
        out_specs=tuple(vmem(2)),
        compiler_params=pltpu.CompilerParams(vmem_limit_bytes=16 << 20),
    )(back, xn, normed, heads_bias)


def totals_kernel(planes_ref, w_ref, wout_ref, wbias_ref, gain_ref):
    scale = 1.0 / N

    def parts(row):
        plane = planes_ref[row].astype(F32) * scale
        return [member(plane, m) for m in range(2)]

    for u in range(2):
        for block in range(4):
            at = slice((block % 2) * W, (block % 2 + 1) * W)
            w_ref[u * 64 : (u + 1) * 64, block * C : (block + 1) * C] = jnp.concatenate(
                [part[:, at] for part in parts(2 * u + block // 2)], axis=1
            )
    for m, part in enumerate(parts(4)):
        wout_ref[m * W : (m + 1) * W] = part
    for h in range(2):
        for m, part in enumerate(parts(5 + h)):
            wbias_ref[2 * m + h : 2 * m + h + 1] = jnp.sum(part, axis=0, keepdims=True)
    gain_ref[...] = jnp.sum(planes_ref[7].astype(F32), axis=0, keepdims=True) * scale


def totals(planes):
    return pl.pallas_call(
        totals_kernel,
        out_shape=(
            jax.ShapeDtypeStruct((C, 4 * C), F32),
            jax.ShapeDtypeStruct((C, C), F32),
            jax.ShapeDtypeStruct((H, C), F32),
            jax.ShapeDtypeStruct((1, C), F32),
        ),
        in_specs=vmem(1),
        out_specs=tuple(vmem(4)),
        compiler_params=pltpu.CompilerParams(vmem_limit_bytes=8 << 20),
    )(planes)


def exchanged(blocks, axes=ROW):
    return lax.all_to_all(blocks, axes, split_axis=0, concat_axis=0, tiled=True)


def per_device(pair, out_grad, w_qkvg, w_out, w_bias, gain):
    sent = pack(pair, gain, w_bias)
    sent, pair, out_grad = lax.optimization_barrier((sent, pair, out_grad))
    mine = lax.axis_index("row_1")
    partner = [(0, 1), (1, 0)]
    cells = pair.reshape(2, 128, 2, C).transpose(0, 2, 1, 3).reshape(4, 128, C)
    grads = out_grad.reshape(128, 2, 2, C).transpose(2, 1, 0, 3).reshape(4, 128, C)
    both = jnp.concatenate([grads, cells], axis=0)
    other = lax.ppermute(both, "row_1", partner)
    first, second = jnp.where(mine == 0, both, other), jnp.where(mine == 0, other, both)
    grads = jnp.concatenate([first[:4], second[:4]], axis=0).reshape(4, N, C)
    xn, normed, inv_std = normalize(jnp.concatenate([first[4:], second[4:]], axis=0), gain)
    heads_bias = lax.dynamic_slice_in_dim(w_bias.T.astype(F32), 2 * mine, 2, axis=0)
    grads, xn, normed, inv_std, gain, heads_bias = lax.optimization_barrier(
        (grads, xn, normed, inv_std, gain, heads_bias)
    )
    w_own = lax.dynamic_index_in_dim(
        w_qkvg.reshape(C, 4, 2, W), mine, axis=2, keepdims=False
    ).reshape(C, 4 * W)
    wout_own = lax.dynamic_slice_in_dim(w_out, mine * W, W, axis=0)
    cols = exchanged(sent).transpose(1, 0, 2)
    planes = attention(cols, grads, w_own, w_own.T, wout_own)
    back = exchanged(planes.transpose(1, 0, 2).reshape(64, 19, 2, C), ("row_0", "row_2"))
    back = back.reshape(64, 38, C).transpose(1, 0, 2)
    last, d_xn = middle(back, xn, normed, heads_bias)
    last, d_xn = lax.optimization_barrier((last, d_xn))
    moved = lax.ppermute(
        jnp.where(mine == 0, d_xn[4:], d_xn[:4]).astype(BF16), "row_1", partner
    )

    def own(planes):
        return jnp.where(mine == 0, planes[:4], planes[4:])

    d_xn, normed, inv_std = own(d_xn) + moved.astype(F32), own(normed), own(inv_std)
    scaled = d_xn * gain
    d_pair = (
        inv_std
        * (
            scaled
            - jnp.mean(scaled, axis=-1, keepdims=True)
            - normed * jnp.mean(scaled * normed, axis=-1, keepdims=True)
        )
    ).astype(BF16)
    d_pair = d_pair.reshape(2, 2, 128, C).transpose(0, 2, 1, 3).reshape(2, N, C)
    d_w, d_wout, d_wbias, d_gain = totals(exchanged(last).transpose(1, 0, 2))
    return d_pair, d_w, d_wout, d_wbias.T, d_gain[0]


def solution(mesh):
    split = Mesh(
        mesh.devices.reshape(mesh.shape["crop"], 8, 2, 8), ("crop", "row_0", "row_1", "row_2")
    )
    placed = (P(CROP_ROW, None, None), P("crop", ROW, None), P(), P(), P(), P())
    return jax.shard_map(
        per_device,
        mesh=split,
        in_specs=placed,
        out_specs=(
            P(CROP_ROW, None, None),
            P("crop", None),
            P("crop", None),
            P("crop", None),
            P("crop"),
        ),
        check_vma=False,
    )
```

```python
import jax
import jax.numpy as jnp
from jax import lax
from jax.experimental import pallas as pl
from jax.experimental.pallas import tpu as pltpu
from jax.sharding import Mesh
from jax.sharding import PartitionSpec as P

DH = 32
H = 4
C = 128
N = 256
DEV = 128
W = 64
SCALE = DH ** (-0.5)
ROW = ("row_0", "row_1", "row_2")
CROP_ROW = ("crop", "row_0", "row_1", "row_2")
EPSILON = 1e-05
LOG2E = 1.4426950408889634
F32 = jnp.float32
BF16 = jnp.bfloat16


def dot(a, b, ca=1, cb=0):
    return lax.dot_general(a, b, (((ca,), (cb,)), ((), ())), preferred_element_type=F32)


def normalize(pair, gain):
    values = pair.astype(F32)
    center = jnp.mean(values, axis=-1, keepdims=True)
    spread = jnp.mean(jnp.square(values - center), axis=-1, keepdims=True)
    inv_std = lax.rsqrt(spread + EPSILON)
    normed = (values - center) * inv_std
    return ((normed * gain).astype(BF16), normed, inv_std)


def doubled(plane, m):
    own = plane.reshape(8, 2, 8, C)[:, m : m + 1]
    return jnp.concatenate([own, own], axis=1).reshape(128, C)


def member(rows, m):
    return rows.reshape(8, 2, 8, -1)[:, m].reshape(64, -1)


def pack_kernel(pair_ref, gain_ref, wbias_ref, out_ref, cells, packed):
    cells[...] = pair_ref[...].reshape(2 * N, C).astype(F32)
    bias = []
    for plane in range(4):
        r, c = plane // 2, plane % 2
        xn, _, _ = normalize(cells[pl.ds(r * N + c, 128, stride=2), :], gain_ref[...])
        bias.append(dot(wbias_ref[...], xn, 1, 1).astype(BF16).astype(F32))
        xn = xn.astype(F32)
        for m in range(2):
            packed[pl.ds(4 * m + plane, 128, stride=8), :] = doubled(xn, m)
    heads = [
        jnp.concatenate(
            [bias[plane][h : h + 1] for h in (2 * m, 2 * m + 1) for plane in range(4)], axis=0
        )
        for m in range(2)
    ]
    rows = jnp.concatenate([jnp.broadcast_to(x[None], (8, 8, C)) for x in heads], axis=0)
    rows = jnp.concatenate([rows] * 8, axis=0)
    out_ref[...] = jnp.concatenate([rows, packed[...].reshape(DEV, 8, C)], axis=1).astype(BF16)


def pack(pair, gain, w_bias):
    return pl.pallas_call(
        pack_kernel,
        out_shape=jax.ShapeDtypeStruct((DEV, 16, C), BF16),
        in_specs=vmem(3),
        out_specs=vmem(1)[0],
        scratch_shapes=[pltpu.VMEM((2 * N, C), F32), pltpu.VMEM((8 * DEV, C), F32)],
    )(pair, gain.reshape(1, C), w_bias.T)


def attention_kernel(cols_ref, grad_ref, w_ref, wt_ref, wout_ref, out_ref):
    def prepare(t):
        at = 8 + 4 * (t // 2) + t % 2
        tokens = jnp.concatenate([cols_ref[at], cols_ref[at + 2]], axis=0)
        grads = grad_ref[t]
        proj = dot(tokens, w_ref[:, : 3 * W]).astype(BF16)
        proj_t = dot(wt_ref[...], tokens, 1, 1)
        gate_t = jax.nn.sigmoid(proj_t[3 * W :])
        d_mixed_t = dot(wout_ref[...], grads, 1, 1)
        d_att_t = (d_mixed_t * gate_t).astype(BF16)
        return dict(
            tokens=tokens,
            grads=grads,
            q=proj[:, :W],
            k=proj[:, W : 2 * W],
            v=proj[:, 2 * W :],
            q_t=proj_t[:W].astype(BF16),
            k_t=proj_t[W : 2 * W].astype(BF16),
            v_t=proj_t[2 * W : 3 * W].astype(BF16),
            gate_t=gate_t,
            d_mixed_t=d_mixed_t,
            d_att_t=d_att_t,
            d_att=d_att_t.T,
            att_h=[],
            dq_h=[],
            d_k=None,
            d_v=None,
        )

    lane = lax.broadcasted_iota(jnp.int32, (N, W), 1) // DH
    zero = jnp.zeros((N, W), BF16)

    def raw(col, h):
        rows = slice(h * DH, (h + 1) * DH)
        s = dot(col["k"][:, rows], col["q_t"][rows])
        d_probs = dot(col["v"][:, rows], col["d_att_t"][rows])
        return s, d_probs

    def head(col, h, bias, s, d_probs):
        own = lane == h
        rows = slice(h * DH, (h + 1) * DH)
        s = s * (SCALE * LOG2E) + bias
        e = jnp.exp2(s - jnp.max(s, axis=0, keepdims=True))
        probs = e * (1.0 / jnp.sum(e, axis=0, keepdims=True))
        probs_b = probs.astype(BF16)
        att_h = dot(col["v_t"][rows], probs_b)
        delta = jnp.sum(col["d_att_t"][rows].astype(F32) * att_h, axis=0, keepdims=True)
        d_s = probs * (d_probs - delta)
        d_sb = d_s.astype(BF16)
        col["att_h"].append(att_h)
        col["dq_h"].append(dot(col["k_t"][rows], d_sb))
        dk_h = dot(d_sb, jnp.where(own, col["q"], zero))
        dv_h = dot(probs_b, jnp.where(own, col["d_att"], zero))
        col["d_k"] = dk_h if h == 0 else col["d_k"] + dk_h
        col["d_v"] = dv_h if h == 0 else col["d_v"] + dv_h
        return d_s

    def finish(col):
        att_t = jnp.concatenate(col["att_h"], axis=0)
        gate_t = col["gate_t"]
        mixed_t = (gate_t * att_t).astype(BF16)
        d_gate_t = (col["d_mixed_t"] * att_t * gate_t * (1.0 - gate_t)).astype(BF16)
        d_q_t = (jnp.concatenate(col["dq_h"], axis=0) * SCALE).astype(BF16)
        d_proj = jnp.concatenate(
            [d_q_t.T, (col["d_k"] * SCALE).astype(BF16), col["d_v"].astype(BF16), d_gate_t.T],
            axis=1,
        )
        d_tokens = dot(d_proj, wt_ref[...])
        return dot(col["tokens"], d_proj, 0, 0), dot(mixed_t, col["grads"]), d_tokens

    def bias_of(h):
        return (
            jnp.concatenate(
                [
                    jnp.concatenate([cols_ref[4 * h + 2 * r], cols_ref[4 * h + 2 * r + 1]], axis=1)
                    for r in range(2)
                ],
                axis=0,
            ).astype(F32)
            * LOG2E
        )

    cols = [prepare(t) for t in range(4)]
    order = [(h, t) for h in range(2) for t in range(4)]
    ahead = raw(cols[0], 0)
    for step, (h, t) in enumerate(order):
        s, d_probs = ahead
        if step + 1 < len(order):
            ahead = raw(cols[order[step + 1][1]], order[step + 1][0])
        if t == 0:
            bias, total = bias_of(h), 0.0
        total = total + head(cols[t], h, bias, s, d_probs)
        if t == 3:
            for r in range(2):
                for m in range(2):
                    part = member(total[r * 128 : (r + 1) * 128], m).astype(BF16)
                    for half in range(2):
                        out_ref[8 * h + 4 * m + 2 * r + half] = part[
                            :, half * 128 : (half + 1) * 128
                        ]
    d_w, d_wout = 0.0, 0.0
    for t in range(4):
        part_w, part_wout, d_tokens = finish(cols[t])
        d_w, d_wout = d_w + part_w, d_wout + part_wout
        for r in range(2):
            for m in range(2):
                at = 16 + 8 * m + 4 * (t // 2) + 2 * r + t % 2
                out_ref[at] = member(d_tokens[r * 128 : (r + 1) * 128], m).astype(BF16)
    d_w = d_w.astype(BF16)
    for u in range(2):
        for block in range(2):
            out_ref[32 + 2 * u + block] = d_w[
                u * 64 : (u + 1) * 64, block * C : (block + 1) * C
            ]
    out_ref[36] = d_wout.astype(BF16)
    out_ref[37] = jnp.zeros((64, C), BF16)


def vmem(count):
    return [pl.BlockSpec(memory_space=pltpu.VMEM)] * count


def attention(cols, grads, w, w_t, w_out):
    return pl.pallas_call(
        attention_kernel,
        out_shape=jax.ShapeDtypeStruct((38, 64, C), BF16),
        in_specs=vmem(5),
        out_specs=vmem(1)[0],
        compiler_params=pltpu.CompilerParams(vmem_limit_bytes=24 << 20),
        cost_estimate=pl.CostEstimate(
            flops=900_000_000, bytes_accessed=3_000_000, transcendentals=600_000
        ),
    )(cols, grads, w, w_t, w_out)


def middle_kernel(back_ref, xn_ref, normed_ref, wbias_ref, out_ref, d_xn_ref):
    def sums(row):
        return jnp.sum(back_ref[row].astype(F32), axis=0, keepdims=True)

    w_three = jnp.concatenate([wbias_ref[...]] * 3, axis=0).astype(BF16)
    d_wbias, d_gain = 0.0, 0.0
    for plane in range(8):
        m, cell = plane // 4, plane % 4
        owned = jnp.concatenate([sums(plane), sums(8 + plane)], axis=0)
        terms = [owned.astype(BF16)]
        left = owned - terms[0].astype(F32)
        terms.append(left.astype(BF16))
        terms.append((left - terms[1].astype(F32)).astype(BF16))
        three = jnp.concatenate(terms, axis=0)
        d_bias_x = dot(three, w_three, 0, 0)
        at = 16 + 8 * m + cell
        d_att_x = jnp.concatenate(
            [back_ref[at + 4 * j].astype(F32).reshape(8, 1, 8, C) for j in range(2)], axis=1
        )
        d_xn = d_att_x.reshape(128, C) + d_bias_x
        d_xn_ref[plane] = d_xn
        d_gain = d_gain + jnp.sum(d_xn * normed_ref[plane], axis=0, keepdims=True)
        parts = dot(three, xn_ref[plane])
        d_wbias = d_wbias + (parts[:2] + parts[2:4] + parts[4:])
    rows = jnp.concatenate([sums(row) for row in range(32, 37)] + [d_wbias, d_gain], axis=0)
    out_ref[...] = jnp.broadcast_to(rows[None], (DEV, 8, C)).astype(BF16)


def middle(back, xn, normed, heads_bias):
    return pl.pallas_call(
        middle_kernel,
        out_shape=(
            jax.ShapeDtypeStruct((DEV, 8, C), BF16),
            jax.ShapeDtypeStruct((8, DEV, C), F32),
        ),
        in_specs=vmem(4),
        out_specs=tuple(vmem(2)),
        compiler_params=pltpu.CompilerParams(vmem_limit_bytes=16 << 20),
    )(back, xn, normed, heads_bias)


def totals_kernel(planes_ref, w_ref, wout_ref, wbias_ref, gain_ref):
    scale = 1.0 / N

    def parts(row):
        plane = planes_ref[row].astype(F32) * scale
        return [member(plane, m) for m in range(2)]

    for u in range(2):
        for block in range(4):
            at = slice((block % 2) * W, (block % 2 + 1) * W)
            w_ref[u * 64 : (u + 1) * 64, block * C : (block + 1) * C] = jnp.concatenate(
                [part[:, at] for part in parts(2 * u + block // 2)], axis=1
            )
    for m, part in enumerate(parts(4)):
        wout_ref[m * W : (m + 1) * W] = part
    for h in range(2):
        for m, part in enumerate(parts(5 + h)):
            wbias_ref[2 * m + h : 2 * m + h + 1] = jnp.sum(part, axis=0, keepdims=True)
    gain_ref[...] = jnp.sum(planes_ref[7].astype(F32), axis=0, keepdims=True) * scale


def totals(planes):
    return pl.pallas_call(
        totals_kernel,
        out_shape=(
            jax.ShapeDtypeStruct((C, 4 * C), F32),
            jax.ShapeDtypeStruct((C, C), F32),
            jax.ShapeDtypeStruct((H, C), F32),
            jax.ShapeDtypeStruct((1, C), F32),
        ),
        in_specs=vmem(1),
        out_specs=tuple(vmem(4)),
        compiler_params=pltpu.CompilerParams(vmem_limit_bytes=8 << 20),
    )(planes)


def exchanged(blocks, axes=ROW):
    return lax.all_to_all(blocks, axes, split_axis=0, concat_axis=0, tiled=True)


def per_device(pair, out_grad, w_qkvg, w_out, w_bias, gain):
    sent = pack(pair, gain, w_bias)
    sent, pair, out_grad = lax.optimization_barrier((sent, pair, out_grad))
    mine = lax.axis_index("row_1")
    partner = [(0, 1), (1, 0)]
    cells = pair.reshape(2, 128, 2, C).transpose(0, 2, 1, 3).reshape(4, 128, C)
    grads = out_grad.reshape(128, 2, 2, C).transpose(2, 1, 0, 3).reshape(4, 128, C)
    both = jnp.concatenate([grads, cells], axis=0)
    other = lax.ppermute(both, "row_1", partner)
    first, second = jnp.where(mine == 0, both, other), jnp.where(mine == 0, other, both)
    grads = jnp.concatenate([first[:4], second[:4]], axis=0).reshape(4, N, C)
    xn, normed, inv_std = normalize(jnp.concatenate([first[4:], second[4:]], axis=0), gain)
    heads_bias = lax.dynamic_slice_in_dim(w_bias.T.astype(F32), 2 * mine, 2, axis=0)
    grads, xn, normed, inv_std, gain, heads_bias = lax.optimization_barrier(
        (grads, xn, normed, inv_std, gain, heads_bias)
    )
    w_own = lax.dynamic_index_in_dim(
        w_qkvg.reshape(C, 4, 2, W), mine, axis=2, keepdims=False
    ).reshape(C, 4 * W)
    wout_own = lax.dynamic_slice_in_dim(w_out, mine * W, W, axis=0)
    cols = exchanged(sent).transpose(1, 0, 2)
    planes = attention(cols, grads, w_own, w_own.T, wout_own)
    back = exchanged(planes.transpose(1, 0, 2).reshape(64, 19, 2, C), ("row_0", "row_2"))
    back = back.reshape(64, 38, C).transpose(1, 0, 2)
    last, d_xn = middle(back, xn, normed, heads_bias)
    last, d_xn = lax.optimization_barrier((last, d_xn))
    arrived = exchanged(last)
    moved = lax.ppermute(jnp.where(mine == 0, d_xn[4:], d_xn[:4]).astype(BF16), "row_1", partner)

    def own(planes):
        return jnp.where(mine == 0, planes[:4], planes[4:])

    d_xn, normed, inv_std = own(d_xn) + moved.astype(F32), own(normed), own(inv_std)
    scaled = d_xn * gain
    d_pair = (
        inv_std
        * (
            scaled
            - jnp.mean(scaled, axis=-1, keepdims=True)
            - normed * jnp.mean(scaled * normed, axis=-1, keepdims=True)
        )
    ).astype(BF16)
    d_pair = d_pair.reshape(2, 2, 128, C).transpose(0, 2, 1, 3).reshape(2, N, C)
    d_w, d_wout, d_wbias, d_gain = totals(arrived.transpose(1, 0, 2))
    return d_pair, d_w, d_wout, d_wbias.T, d_gain[0]


def solution(mesh):
    split = Mesh(
        mesh.devices.reshape(mesh.shape["crop"], 8, 2, 8), ("crop", "row_0", "row_1", "row_2")
    )
    placed = (P(CROP_ROW, None, None), P("crop", ROW, None), P(), P(), P(), P())
    return jax.shard_map(
        per_device,
        mesh=split,
        in_specs=placed,
        out_specs=(
            P(CROP_ROW, None, None),
            P("crop", None),
            P("crop", None),
            P("crop", None),
            P("crop"),
        ),
        check_vma=False,
    )
```

```python
import jax
import jax.numpy as jnp
from jax import lax
from jax.experimental import pallas as pl
from jax.experimental.pallas import tpu as pltpu
from jax.sharding import Mesh
from jax.sharding import PartitionSpec as P

DH = 32
H = 4
C = 128
N = 256
DEV = 128
W = 64
SCALE = DH ** (-0.5)
ROW = ("row_0", "row_1", "row_2")
CROP_ROW = ("crop", "row_0", "row_1", "row_2")
EPSILON = 1e-05
LOG2E = 1.4426950408889634
F32 = jnp.float32
BF16 = jnp.bfloat16


def dot(a, b, ca=1, cb=0):
    return lax.dot_general(a, b, (((ca,), (cb,)), ((), ())), preferred_element_type=F32)


def normalize(pair, gain):
    values = pair.astype(F32)
    center = jnp.mean(values, axis=-1, keepdims=True)
    spread = jnp.mean(jnp.square(values - center), axis=-1, keepdims=True)
    inv_std = lax.rsqrt(spread + EPSILON)
    normed = (values - center) * inv_std
    return ((normed * gain).astype(BF16), normed, inv_std)


def doubled(plane, m):
    own = plane.reshape(8, 2, 8, C)[:, m : m + 1]
    return jnp.concatenate([own, own], axis=1).reshape(128, C)


def member(rows, m):
    return rows.reshape(8, 2, 8, -1)[:, m].reshape(64, -1)


def pack_kernel(pair_ref, gain_ref, wbias_ref, out_ref, cells, packed):
    cells[...] = pair_ref[...].reshape(2 * N, C).astype(F32)
    bias = []
    for plane in range(4):
        r, c = plane // 2, plane % 2
        xn, _, _ = normalize(cells[pl.ds(r * N + c, 128, stride=2), :], gain_ref[...])
        bias.append(dot(wbias_ref[...], xn, 1, 1).astype(BF16).astype(F32))
        xn = xn.astype(F32)
        for m in range(2):
            packed[pl.ds(4 * m + plane, 128, stride=8), :] = doubled(xn, m)
    heads = [
        jnp.concatenate(
            [bias[plane][h : h + 1] for h in (2 * m, 2 * m + 1) for plane in range(4)], axis=0
        )
        for m in range(2)
    ]
    rows = jnp.concatenate([jnp.broadcast_to(x[None], (8, 8, C)) for x in heads], axis=0)
    rows = jnp.concatenate([rows] * 8, axis=0)
    out_ref[...] = jnp.concatenate([rows, packed[...].reshape(DEV, 8, C)], axis=1).astype(BF16)


def pack(pair, gain, w_bias):
    return pl.pallas_call(
        pack_kernel,
        out_shape=jax.ShapeDtypeStruct((DEV, 16, C), BF16),
        in_specs=vmem(3),
        out_specs=vmem(1)[0],
        scratch_shapes=[pltpu.VMEM((2 * N, C), F32), pltpu.VMEM((8 * DEV, C), F32)],
    )(pair, gain.reshape(1, C), w_bias.T)


def attention_kernel(cols_ref, grad_ref, w_ref, wt_ref, wout_ref, out_ref):
    def prepare(t):
        at = 8 + 4 * (t // 2) + t % 2
        tokens = jnp.concatenate([cols_ref[at], cols_ref[at + 2]], axis=0)
        grads = grad_ref[t]
        proj = dot(tokens, w_ref[:, : 3 * W]).astype(BF16)
        proj_t = dot(wt_ref[...], tokens, 1, 1)
        gate_t = jax.nn.sigmoid(proj_t[3 * W :])
        d_mixed_t = dot(wout_ref[...], grads, 1, 1)
        d_att_t = (d_mixed_t * gate_t).astype(BF16)
        return dict(
            tokens=tokens,
            grads=grads,
            q=proj[:, :W],
            k=proj[:, W : 2 * W],
            v=proj[:, 2 * W :],
            q_t=proj_t[:W].astype(BF16),
            k_t=proj_t[W : 2 * W].astype(BF16),
            v_t=proj_t[2 * W : 3 * W].astype(BF16),
            gate_t=gate_t,
            d_mixed_t=d_mixed_t,
            d_att_t=d_att_t,
            d_att=d_att_t.T,
            att_h=[],
            dq_h=[],
            d_k=None,
            d_v=None,
        )

    lane = lax.broadcasted_iota(jnp.int32, (N, W), 1) // DH
    zero = jnp.zeros((N, W), BF16)

    def raw(col, h):
        rows = slice(h * DH, (h + 1) * DH)
        s = dot(col["k"][:, rows], col["q_t"][rows])
        d_probs = dot(col["v"][:, rows], col["d_att_t"][rows])
        return s, d_probs

    def head(col, h, bias, s, d_probs):
        own = lane == h
        rows = slice(h * DH, (h + 1) * DH)
        s = s * (SCALE * LOG2E) + bias
        e = jnp.exp2(s - jnp.max(s, axis=0, keepdims=True))
        probs = e * (1.0 / jnp.sum(e, axis=0, keepdims=True))
        probs_b = probs.astype(BF16)
        att_h = dot(col["v_t"][rows], probs_b)
        delta = jnp.sum(col["d_att_t"][rows].astype(F32) * att_h, axis=0, keepdims=True)
        d_s = probs * (d_probs - delta)
        d_sb = d_s.astype(BF16)
        col["att_h"].append(att_h)
        col["dq_h"].append(dot(col["k_t"][rows], d_sb))
        dk_h = dot(d_sb, jnp.where(own, col["q"], zero))
        dv_h = dot(probs_b, jnp.where(own, col["d_att"], zero))
        col["d_k"] = dk_h if h == 0 else col["d_k"] + dk_h
        col["d_v"] = dv_h if h == 0 else col["d_v"] + dv_h
        return d_s

    def finish(col):
        att_t = jnp.concatenate(col["att_h"], axis=0)
        gate_t = col["gate_t"]
        mixed_t = (gate_t * att_t).astype(BF16)
        d_gate_t = (col["d_mixed_t"] * att_t * gate_t * (1.0 - gate_t)).astype(BF16)
        d_q_t = (jnp.concatenate(col["dq_h"], axis=0) * SCALE).astype(BF16)
        d_proj = jnp.concatenate(
            [d_q_t.T, (col["d_k"] * SCALE).astype(BF16), col["d_v"].astype(BF16), d_gate_t.T],
            axis=1,
        )
        d_tokens = dot(d_proj, wt_ref[...])
        return dot(col["tokens"], d_proj, 0, 0), dot(mixed_t, col["grads"]), d_tokens

    def bias_of(h):
        return (
            jnp.concatenate(
                [
                    jnp.concatenate([cols_ref[4 * h + 2 * r], cols_ref[4 * h + 2 * r + 1]], axis=1)
                    for r in range(2)
                ],
                axis=0,
            ).astype(F32)
            * LOG2E
        )

    cols = [prepare(t) for t in range(4)]
    order = [(h, t) for h in range(2) for t in range(4)]
    ahead = raw(cols[0], 0)
    for step, (h, t) in enumerate(order):
        s, d_probs = ahead
        if step + 1 < len(order):
            ahead = raw(cols[order[step + 1][1]], order[step + 1][0])
        if t == 0:
            bias, total = bias_of(h), 0.0
        total = total + head(cols[t], h, bias, s, d_probs)
        if t == 3:
            for r in range(2):
                for m in range(2):
                    part = member(total[r * 128 : (r + 1) * 128], m).astype(BF16)
                    for half in range(2):
                        out_ref[8 * h + 4 * m + 2 * r + half] = part[
                            :, half * 128 : (half + 1) * 128
                        ]
    d_w, d_wout = 0.0, 0.0
    for t in range(4):
        part_w, part_wout, d_tokens = finish(cols[t])
        d_w, d_wout = d_w + part_w, d_wout + part_wout
        for r in range(2):
            for m in range(2):
                at = 16 + 8 * m + 4 * (t // 2) + 2 * r + t % 2
                out_ref[at] = member(d_tokens[r * 128 : (r + 1) * 128], m).astype(BF16)
    d_w = d_w.astype(BF16)
    for u in range(2):
        for block in range(2):
            out_ref[32 + 2 * u + block] = d_w[
                u * 64 : (u + 1) * 64, block * C : (block + 1) * C
            ]
    out_ref[36] = d_wout.astype(BF16)
    out_ref[37] = jnp.zeros((64, C), BF16)


def vmem(count):
    return [pl.BlockSpec(memory_space=pltpu.VMEM)] * count


def attention(cols, grads, w, w_t, w_out):
    return pl.pallas_call(
        attention_kernel,
        out_shape=jax.ShapeDtypeStruct((38, 64, C), BF16),
        in_specs=vmem(5),
        out_specs=vmem(1)[0],
        compiler_params=pltpu.CompilerParams(vmem_limit_bytes=24 << 20),
        cost_estimate=pl.CostEstimate(
            flops=900_000_000, bytes_accessed=3_000_000, transcendentals=600_000
        ),
    )(cols, grads, w, w_t, w_out)


def middle_kernel(back_ref, cells_ref, rows_ref, out_ref, d_xn_ref):
    def sums(row):
        return jnp.sum(back_ref[row].astype(F32), axis=0, keepdims=True)

    w_three = jnp.concatenate([rows_ref[:2]] * 3, axis=0).astype(BF16)
    d_wbias, d_gain = 0.0, 0.0
    for plane in range(8):
        m, cell = plane // 4, plane % 4
        xn, normed, _ = normalize(cells_ref[plane], rows_ref[2:3])
        owned = jnp.concatenate([sums(plane), sums(8 + plane)], axis=0)
        terms = [owned.astype(BF16)]
        left = owned - terms[0].astype(F32)
        terms.append(left.astype(BF16))
        terms.append((left - terms[1].astype(F32)).astype(BF16))
        three = jnp.concatenate(terms, axis=0)
        d_bias_x = dot(three, w_three, 0, 0)
        at = 16 + 8 * m + cell
        d_att_x = jnp.concatenate(
            [back_ref[at + 4 * j].astype(F32).reshape(8, 1, 8, C) for j in range(2)], axis=1
        )
        d_xn = d_att_x.reshape(128, C) + d_bias_x
        d_xn_ref[plane] = d_xn
        d_gain = d_gain + jnp.sum(d_xn * normed, axis=0, keepdims=True)
        parts = dot(three, xn)
        d_wbias = d_wbias + (parts[:2] + parts[2:4] + parts[4:])
    rows = jnp.concatenate([sums(row) for row in range(32, 37)] + [d_wbias, d_gain], axis=0)
    out_ref[...] = jnp.broadcast_to(rows[None], (DEV, 8, C)).astype(BF16)


def middle(back, cells, rows):
    return pl.pallas_call(
        middle_kernel,
        out_shape=(
            jax.ShapeDtypeStruct((DEV, 8, C), BF16),
            jax.ShapeDtypeStruct((8, DEV, C), F32),
        ),
        in_specs=vmem(3),
        out_specs=tuple(vmem(2)),
        compiler_params=pltpu.CompilerParams(vmem_limit_bytes=16 << 20),
    )(back, cells, rows)


def totals_kernel(planes_ref, w_ref, wout_ref, wbias_ref, gain_ref):
    scale = 1.0 / N

    def parts(row):
        plane = planes_ref[row].astype(F32) * scale
        return [member(plane, m) for m in range(2)]

    for u in range(2):
        for block in range(4):
            at = slice((block % 2) * W, (block % 2 + 1) * W)
            w_ref[u * 64 : (u + 1) * 64, block * C : (block + 1) * C] = jnp.concatenate(
                [part[:, at] for part in parts(2 * u + block // 2)], axis=1
            )
    for m, part in enumerate(parts(4)):
        wout_ref[m * W : (m + 1) * W] = part
    for h in range(2):
        for m, part in enumerate(parts(5 + h)):
            wbias_ref[2 * m + h : 2 * m + h + 1] = jnp.sum(part, axis=0, keepdims=True)
    gain_ref[...] = jnp.sum(planes_ref[7].astype(F32), axis=0, keepdims=True) * scale


def totals(planes):
    return pl.pallas_call(
        totals_kernel,
        out_shape=(
            jax.ShapeDtypeStruct((C, 4 * C), F32),
            jax.ShapeDtypeStruct((C, C), F32),
            jax.ShapeDtypeStruct((H, C), F32),
            jax.ShapeDtypeStruct((1, C), F32),
        ),
        in_specs=vmem(1),
        out_specs=tuple(vmem(4)),
        compiler_params=pltpu.CompilerParams(vmem_limit_bytes=8 << 20),
    )(planes)


def exchanged(blocks, axes=ROW):
    return lax.all_to_all(blocks, axes, split_axis=0, concat_axis=0, tiled=True)


def per_device(pair, out_grad, w_qkvg, w_out, w_bias, gain):
    sent = pack(pair, gain, w_bias)
    sent, pair, out_grad = lax.optimization_barrier((sent, pair, out_grad))
    mine = lax.axis_index("row_1")
    partner = [(0, 1), (1, 0)]
    cells = pair.reshape(2, 128, 2, C).transpose(0, 2, 1, 3).reshape(4, 128, C)
    grads = out_grad.reshape(128, 2, 2, C).transpose(2, 1, 0, 3).reshape(4, 128, C)

    def in_order(own, other):
        first, second = jnp.where(mine == 0, own, other), jnp.where(mine == 0, other, own)
        return jnp.concatenate([first, second], axis=0)

    other = lax.ppermute(jnp.concatenate([grads, cells], axis=0), "row_1", partner)
    grads = in_order(grads, other[:4]).reshape(4, N, C)
    pair_cells = in_order(cells, other[4:])
    rows = lax.dynamic_slice_in_dim(w_bias.T.astype(F32), 2 * mine, 2, axis=0)
    rows = jnp.concatenate([rows, gain[None]], axis=0)
    grads, pair_cells, rows = lax.optimization_barrier((grads, pair_cells, rows))
    w_own = lax.dynamic_index_in_dim(
        w_qkvg.reshape(C, 4, 2, W), mine, axis=2, keepdims=False
    ).reshape(C, 4 * W)
    wout_own = lax.dynamic_slice_in_dim(w_out, mine * W, W, axis=0)
    cols = exchanged(sent).transpose(1, 0, 2)
    planes = attention(cols, grads, w_own, w_own.T, wout_own)
    back = exchanged(planes.transpose(1, 0, 2).reshape(64, 19, 2, C), ("row_0", "row_2"))
    back = back.reshape(64, 38, C).transpose(1, 0, 2)
    last, d_xn = middle(back, pair_cells, rows)
    last, d_xn = lax.optimization_barrier((last, d_xn))
    arrived = exchanged(last)
    moved = lax.ppermute(jnp.where(mine == 0, d_xn[4:], d_xn[:4]).astype(BF16), "row_1", partner)

    moved, cells = lax.optimization_barrier((moved, cells))
    _, normed, inv_std = normalize(cells, gain)
    d_xn = jnp.where(mine == 0, d_xn[:4], d_xn[4:]) + moved.astype(F32)
    scaled = d_xn * gain
    d_pair = (
        inv_std
        * (
            scaled
            - jnp.mean(scaled, axis=-1, keepdims=True)
            - normed * jnp.mean(scaled * normed, axis=-1, keepdims=True)
        )
    ).astype(BF16)
    d_pair = d_pair.reshape(2, 2, 128, C).transpose(0, 2, 1, 3).reshape(2, N, C)
    d_w, d_wout, d_wbias, d_gain = totals(arrived.transpose(1, 0, 2))
    return d_pair, d_w, d_wout, d_wbias.T, d_gain[0]


def solution(mesh):
    split = Mesh(
        mesh.devices.reshape(mesh.shape["crop"], 8, 2, 8), ("crop", "row_0", "row_1", "row_2")
    )
    placed = (P(CROP_ROW, None, None), P("crop", ROW, None), P(), P(), P(), P())
    return jax.shard_map(
        per_device,
        mesh=split,
        in_specs=placed,
        out_specs=(
            P(CROP_ROW, None, None),
            P("crop", None),
            P("crop", None),
            P("crop", None),
            P("crop"),
        ),
        check_vma=False,
    )
```

```python
import jax
import jax.numpy as jnp
from jax import lax
from jax.experimental import pallas as pl
from jax.experimental.pallas import tpu as pltpu
from jax.sharding import Mesh
from jax.sharding import PartitionSpec as P

DH = 32
H = 4
C = 128
N = 256
DEV = 128
W = 64
SCALE = DH ** (-0.5)
ROW = ("row_0", "row_1", "row_2")
CROP_ROW = ("crop", "row_0", "row_1", "row_2")
EPSILON = 1e-05
LOG2E = 1.4426950408889634
F32 = jnp.float32
BF16 = jnp.bfloat16


def dot(a, b, ca=1, cb=0):
    return lax.dot_general(a, b, (((ca,), (cb,)), ((), ())), preferred_element_type=F32)


def normalize(pair, gain):
    values = pair.astype(F32)
    center = jnp.mean(values, axis=-1, keepdims=True)
    spread = jnp.mean(jnp.square(values - center), axis=-1, keepdims=True)
    inv_std = lax.rsqrt(spread + EPSILON)
    normed = (values - center) * inv_std
    return ((normed * gain).astype(BF16), normed, inv_std)


def doubled(plane, m):
    own = plane.reshape(8, 2, 8, C)[:, m : m + 1]
    return jnp.concatenate([own, own], axis=1).reshape(128, C)


def member(rows, m):
    return rows.reshape(8, 2, 8, -1)[:, m].reshape(64, -1)


def pack_kernel(pair_ref, gain_ref, wbias_ref, out_ref, cells, packed):
    cells[...] = pair_ref[...].reshape(2 * N, C).astype(F32)
    bias = []
    for plane in range(4):
        r, c = plane // 2, plane % 2
        xn, _, _ = normalize(cells[pl.ds(r * N + c, 128, stride=2), :], gain_ref[...])
        bias.append(dot(wbias_ref[...], xn, 1, 1).astype(BF16).astype(F32))
        xn = xn.astype(F32)
        for m in range(2):
            packed[pl.ds(4 * m + plane, 128, stride=8), :] = doubled(xn, m)
    heads = [
        jnp.concatenate(
            [bias[plane][h : h + 1] for h in (2 * m, 2 * m + 1) for plane in range(4)], axis=0
        )
        for m in range(2)
    ]
    rows = jnp.concatenate([jnp.broadcast_to(x[None], (8, 8, C)) for x in heads], axis=0)
    rows = jnp.concatenate([rows] * 8, axis=0)
    out_ref[...] = jnp.concatenate([rows, packed[...].reshape(DEV, 8, C)], axis=1).astype(BF16)


def pack(pair, gain, w_bias):
    return pl.pallas_call(
        pack_kernel,
        out_shape=jax.ShapeDtypeStruct((DEV, 16, C), BF16),
        in_specs=vmem(3),
        out_specs=vmem(1)[0],
        scratch_shapes=[pltpu.VMEM((2 * N, C), F32), pltpu.VMEM((8 * DEV, C), F32)],
    )(pair, gain.reshape(1, C), w_bias.T)


def attention_kernel(cols_ref, grad_ref, w_ref, wt_ref, wout_ref, out_ref):
    def prepare(t):
        at = 8 + 4 * (t // 2) + t % 2
        tokens = jnp.concatenate([cols_ref[at], cols_ref[at + 2]], axis=0)
        grads = grad_ref[t]
        proj = dot(tokens, w_ref[:, : 3 * W]).astype(BF16)
        proj_t = dot(wt_ref[...], tokens, 1, 1)
        gate_t = jax.nn.sigmoid(proj_t[3 * W :])
        d_mixed_t = dot(wout_ref[...], grads, 1, 1)
        d_att_t = (d_mixed_t * gate_t).astype(BF16)
        return dict(
            tokens=tokens,
            grads=grads,
            q=proj[:, :W],
            k=proj[:, W : 2 * W],
            v=proj[:, 2 * W :],
            q_t=proj_t[:W].astype(BF16),
            k_t=proj_t[W : 2 * W].astype(BF16),
            v_t=proj_t[2 * W : 3 * W].astype(BF16),
            gate_t=gate_t,
            d_mixed_t=d_mixed_t,
            d_att_t=d_att_t,
            d_att=d_att_t.T,
            att_h=[],
            dq_h=[],
            d_k=None,
            d_v=None,
        )

    lane = lax.broadcasted_iota(jnp.int32, (N, W), 1) // DH
    zero = jnp.zeros((N, W), BF16)

    def raw(col, h):
        rows = slice(h * DH, (h + 1) * DH)
        s = dot(col["k"][:, rows], col["q_t"][rows])
        d_probs = dot(col["v"][:, rows], col["d_att_t"][rows])
        return s, d_probs

    def head(col, h, bias, s, d_probs):
        own = lane == h
        rows = slice(h * DH, (h + 1) * DH)
        s = s * (SCALE * LOG2E) + bias
        e = jnp.exp2(s - jnp.max(s, axis=0, keepdims=True))
        probs = e * (1.0 / jnp.sum(e, axis=0, keepdims=True))
        probs_b = probs.astype(BF16)
        att_h = dot(col["v_t"][rows], probs_b)
        delta = jnp.sum(col["d_att_t"][rows].astype(F32) * att_h, axis=0, keepdims=True)
        d_s = probs * (d_probs - delta)
        d_sb = d_s.astype(BF16)
        col["att_h"].append(att_h)
        col["dq_h"].append(dot(col["k_t"][rows], d_sb))
        dk_h = dot(d_sb, jnp.where(own, col["q"], zero))
        dv_h = dot(probs_b, jnp.where(own, col["d_att"], zero))
        col["d_k"] = dk_h if h == 0 else col["d_k"] + dk_h
        col["d_v"] = dv_h if h == 0 else col["d_v"] + dv_h
        return d_s

    def finish(col):
        att_t = jnp.concatenate(col["att_h"], axis=0)
        gate_t = col["gate_t"]
        mixed_t = (gate_t * att_t).astype(BF16)
        d_gate_t = (col["d_mixed_t"] * att_t * gate_t * (1.0 - gate_t)).astype(BF16)
        d_q_t = (jnp.concatenate(col["dq_h"], axis=0) * SCALE).astype(BF16)
        d_proj = jnp.concatenate(
            [d_q_t.T, (col["d_k"] * SCALE).astype(BF16), col["d_v"].astype(BF16), d_gate_t.T],
            axis=1,
        )
        d_tokens = dot(d_proj, wt_ref[...])
        return dot(col["tokens"], d_proj, 0, 0), dot(mixed_t, col["grads"]), d_tokens

    def bias_of(h):
        return (
            jnp.concatenate(
                [
                    jnp.concatenate([cols_ref[4 * h + 2 * r], cols_ref[4 * h + 2 * r + 1]], axis=1)
                    for r in range(2)
                ],
                axis=0,
            ).astype(F32)
            * LOG2E
        )

    cols = [prepare(t) for t in range(4)]
    order = [(h, t) for h in range(2) for t in range(4)]
    ahead = [raw(cols[t], h) for h, t in order[:2]]
    for step, (h, t) in enumerate(order):
        s, d_probs = ahead.pop(0)
        if step + 2 < len(order):
            ahead.append(raw(cols[order[step + 2][1]], order[step + 2][0]))
        if t == 0:
            bias, total = bias_of(h), 0.0
        total = total + head(cols[t], h, bias, s, d_probs)
        if t == 3:
            for r in range(2):
                for m in range(2):
                    part = member(total[r * 128 : (r + 1) * 128], m).astype(BF16)
                    for half in range(2):
                        out_ref[8 * h + 4 * m + 2 * r + half] = part[
                            :, half * 128 : (half + 1) * 128
                        ]
    d_w, d_wout = 0.0, 0.0
    for t in range(4):
        part_w, part_wout, d_tokens = finish(cols[t])
        d_w, d_wout = d_w + part_w, d_wout + part_wout
        for r in range(2):
            for m in range(2):
                at = 16 + 8 * m + 4 * (t // 2) + 2 * r + t % 2
                out_ref[at] = member(d_tokens[r * 128 : (r + 1) * 128], m).astype(BF16)
    d_w = d_w.astype(BF16)
    for u in range(2):
        for block in range(2):
            out_ref[32 + 2 * u + block] = d_w[
                u * 64 : (u + 1) * 64, block * C : (block + 1) * C
            ]
    out_ref[36] = d_wout.astype(BF16)
    out_ref[37] = jnp.zeros((64, C), BF16)


def vmem(count):
    return [pl.BlockSpec(memory_space=pltpu.VMEM)] * count


def attention(cols, grads, w, w_t, w_out):
    return pl.pallas_call(
        attention_kernel,
        out_shape=jax.ShapeDtypeStruct((38, 64, C), BF16),
        in_specs=vmem(5),
        out_specs=vmem(1)[0],
        compiler_params=pltpu.CompilerParams(vmem_limit_bytes=24 << 20),
        cost_estimate=pl.CostEstimate(
            flops=900_000_000, bytes_accessed=3_000_000, transcendentals=600_000
        ),
    )(cols, grads, w, w_t, w_out)


def middle_kernel(back_ref, cells_ref, rows_ref, out_ref, d_xn_ref):
    def sums(row):
        return jnp.sum(back_ref[row].astype(F32), axis=0, keepdims=True)

    w_three = jnp.concatenate([rows_ref[:2]] * 3, axis=0).astype(BF16)
    d_wbias, d_gain = 0.0, 0.0
    for plane in range(8):
        m, cell = plane // 4, plane % 4
        xn, normed, _ = normalize(cells_ref[plane], rows_ref[2:3])
        owned = jnp.concatenate([sums(plane), sums(8 + plane)], axis=0)
        terms = [owned.astype(BF16)]
        left = owned - terms[0].astype(F32)
        terms.append(left.astype(BF16))
        terms.append((left - terms[1].astype(F32)).astype(BF16))
        three = jnp.concatenate(terms, axis=0)
        d_bias_x = dot(three, w_three, 0, 0)
        at = 16 + 8 * m + cell
        d_att_x = jnp.concatenate(
            [back_ref[at + 4 * j].astype(F32).reshape(8, 1, 8, C) for j in range(2)], axis=1
        )
        d_xn = d_att_x.reshape(128, C) + d_bias_x
        d_xn_ref[plane] = d_xn
        d_gain = d_gain + jnp.sum(d_xn * normed, axis=0, keepdims=True)
        parts = dot(three, xn)
        d_wbias = d_wbias + (parts[:2] + parts[2:4] + parts[4:])
    rows = jnp.concatenate([sums(row) for row in range(32, 37)] + [d_wbias, d_gain], axis=0)
    out_ref[...] = jnp.broadcast_to(rows[None], (DEV, 8, C)).astype(BF16)


def middle(back, cells, rows):
    return pl.pallas_call(
        middle_kernel,
        out_shape=(
            jax.ShapeDtypeStruct((DEV, 8, C), BF16),
            jax.ShapeDtypeStruct((8, DEV, C), F32),
        ),
        in_specs=vmem(3),
        out_specs=tuple(vmem(2)),
        compiler_params=pltpu.CompilerParams(vmem_limit_bytes=16 << 20),
    )(back, cells, rows)


def totals_kernel(planes_ref, w_ref, wout_ref, wbias_ref, gain_ref):
    scale = 1.0 / N

    def parts(row):
        plane = planes_ref[row].astype(F32) * scale
        return [member(plane, m) for m in range(2)]

    for u in range(2):
        for block in range(4):
            at = slice((block % 2) * W, (block % 2 + 1) * W)
            w_ref[u * 64 : (u + 1) * 64, block * C : (block + 1) * C] = jnp.concatenate(
                [part[:, at] for part in parts(2 * u + block // 2)], axis=1
            )
    for m, part in enumerate(parts(4)):
        wout_ref[m * W : (m + 1) * W] = part
    for h in range(2):
        for m, part in enumerate(parts(5 + h)):
            wbias_ref[2 * m + h : 2 * m + h + 1] = jnp.sum(part, axis=0, keepdims=True)
    gain_ref[...] = jnp.sum(planes_ref[7].astype(F32), axis=0, keepdims=True) * scale


def totals(planes):
    return pl.pallas_call(
        totals_kernel,
        out_shape=(
            jax.ShapeDtypeStruct((C, 4 * C), F32),
            jax.ShapeDtypeStruct((C, C), F32),
            jax.ShapeDtypeStruct((H, C), F32),
            jax.ShapeDtypeStruct((1, C), F32),
        ),
        in_specs=vmem(1),
        out_specs=tuple(vmem(4)),
        compiler_params=pltpu.CompilerParams(vmem_limit_bytes=8 << 20),
    )(planes)


def exchanged(blocks, axes=ROW):
    return lax.all_to_all(blocks, axes, split_axis=0, concat_axis=0, tiled=True)


def per_device(pair, out_grad, w_qkvg, w_out, w_bias, gain):
    sent = pack(pair, gain, w_bias)
    sent, pair, out_grad = lax.optimization_barrier((sent, pair, out_grad))
    mine = lax.axis_index("row_1")
    partner = [(0, 1), (1, 0)]
    cells = pair.reshape(2, 128, 2, C).transpose(0, 2, 1, 3).reshape(4, 128, C)
    grads = out_grad.reshape(128, 2, 2, C).transpose(2, 1, 0, 3).reshape(4, 128, C)

    def in_order(own, other):
        first, second = jnp.where(mine == 0, own, other), jnp.where(mine == 0, other, own)
        return jnp.concatenate([first, second], axis=0)

    other = lax.ppermute(jnp.concatenate([grads, cells], axis=0), "row_1", partner)
    grads = in_order(grads, other[:4]).reshape(4, N, C)
    pair_cells = in_order(cells, other[4:])
    rows = lax.dynamic_slice_in_dim(w_bias.T.astype(F32), 2 * mine, 2, axis=0)
    rows = jnp.concatenate([rows, gain[None]], axis=0)
    grads, pair_cells, rows = lax.optimization_barrier((grads, pair_cells, rows))
    w_own = lax.dynamic_index_in_dim(
        w_qkvg.reshape(C, 4, 2, W), mine, axis=2, keepdims=False
    ).reshape(C, 4 * W)
    wout_own = lax.dynamic_slice_in_dim(w_out, mine * W, W, axis=0)
    cols = exchanged(sent).transpose(1, 0, 2)
    planes = attention(cols, grads, w_own, w_own.T, wout_own)
    back = exchanged(planes.transpose(1, 0, 2).reshape(64, 19, 2, C), ("row_0", "row_2"))
    back = back.reshape(64, 38, C).transpose(1, 0, 2)
    last, d_xn = middle(back, pair_cells, rows)
    last, d_xn = lax.optimization_barrier((last, d_xn))
    arrived = exchanged(last)
    moved = lax.ppermute(jnp.where(mine == 0, d_xn[4:], d_xn[:4]).astype(BF16), "row_1", partner)

    moved, cells = lax.optimization_barrier((moved, cells))
    _, normed, inv_std = normalize(cells, gain)
    d_xn = jnp.where(mine == 0, d_xn[:4], d_xn[4:]) + moved.astype(F32)
    scaled = d_xn * gain
    d_pair = (
        inv_std
        * (
            scaled
            - jnp.mean(scaled, axis=-1, keepdims=True)
            - normed * jnp.mean(scaled * normed, axis=-1, keepdims=True)
        )
    ).astype(BF16)
    d_pair = d_pair.reshape(2, 2, 128, C).transpose(0, 2, 1, 3).reshape(2, N, C)
    d_w, d_wout, d_wbias, d_gain = totals(arrived.transpose(1, 0, 2))
    return d_pair, d_w, d_wout, d_wbias.T, d_gain[0]


def solution(mesh):
    split = Mesh(
        mesh.devices.reshape(mesh.shape["crop"], 8, 2, 8), ("crop", "row_0", "row_1", "row_2")
    )
    placed = (P(CROP_ROW, None, None), P("crop", ROW, None), P(), P(), P(), P())
    return jax.shard_map(
        per_device,
        mesh=split,
        in_specs=placed,
        out_specs=(
            P(CROP_ROW, None, None),
            P("crop", None),
            P("crop", None),
            P("crop", None),
            P("crop"),
        ),
        check_vma=False,
    )
```

```python
import jax
import jax.numpy as jnp
from jax import lax
from jax.experimental import pallas as pl
from jax.experimental.pallas import tpu as pltpu
from jax.sharding import Mesh
from jax.sharding import PartitionSpec as P

DH = 32
H = 4
C = 128
N = 256
DEV = 128
W = 64
SCALE = DH ** (-0.5)
ROW = ("row_0", "row_1", "row_2")
CROP_ROW = ("crop", "row_0", "row_1", "row_2")
EPSILON = 1e-05
LOG2E = 1.4426950408889634
F32 = jnp.float32
BF16 = jnp.bfloat16


def dot(a, b, ca=1, cb=0):
    return lax.dot_general(a, b, (((ca,), (cb,)), ((), ())), preferred_element_type=F32)


def normalize(pair, gain):
    values = pair.astype(F32)
    center = jnp.mean(values, axis=-1, keepdims=True)
    spread = jnp.mean(jnp.square(values - center), axis=-1, keepdims=True)
    inv_std = lax.rsqrt(spread + EPSILON)
    normed = (values - center) * inv_std
    return ((normed * gain).astype(BF16), normed, inv_std)


def doubled(plane, m):
    own = plane.reshape(8, 2, 8, C)[:, m : m + 1]
    return jnp.concatenate([own, own], axis=1).reshape(128, C)


def member(rows, m):
    return rows.reshape(8, 2, 8, -1)[:, m].reshape(64, -1)


def pack_kernel(pair_ref, gain_ref, wbias_ref, out_ref, cells, packed):
    cells[...] = pair_ref[...].reshape(2 * N, C).astype(F32)
    bias = []
    for plane in range(4):
        r, c = plane // 2, plane % 2
        xn, _, _ = normalize(cells[pl.ds(r * N + c, 128, stride=2), :], gain_ref[...])
        bias.append(dot(wbias_ref[...], xn, 1, 1).astype(BF16).astype(F32))
        xn = xn.astype(F32)
        for m in range(2):
            packed[pl.ds(4 * m + plane, 128, stride=8), :] = doubled(xn, m)
    heads = [
        jnp.concatenate(
            [bias[plane][h : h + 1] for h in (2 * m, 2 * m + 1) for plane in range(4)], axis=0
        )
        for m in range(2)
    ]
    rows = jnp.concatenate([jnp.broadcast_to(x[None], (8, 8, C)) for x in heads], axis=0)
    rows = jnp.concatenate([rows] * 8, axis=0)
    out_ref[...] = jnp.concatenate([rows, packed[...].reshape(DEV, 8, C)], axis=1).astype(BF16)


def pack(pair, gain, w_bias):
    return pl.pallas_call(
        pack_kernel,
        out_shape=jax.ShapeDtypeStruct((DEV, 16, C), BF16),
        in_specs=vmem(3),
        out_specs=vmem(1)[0],
        scratch_shapes=[pltpu.VMEM((2 * N, C), F32), pltpu.VMEM((8 * DEV, C), F32)],
    )(pair, gain.reshape(1, C), w_bias.T)


def attention_kernel(cols_ref, grad_ref, w_ref, wt_ref, wout_ref, out_ref):
    def prepare(t):
        at = 8 + 4 * (t // 2) + t % 2
        tokens = jnp.concatenate([cols_ref[at], cols_ref[at + 2]], axis=0)
        grads = grad_ref[t]
        proj = dot(tokens, w_ref[:, : 3 * W]).astype(BF16)
        proj_t = dot(wt_ref[...], tokens, 1, 1)
        gate_t = jax.nn.sigmoid(proj_t[3 * W :])
        d_mixed_t = dot(wout_ref[...], grads, 1, 1)
        d_att_t = (d_mixed_t * gate_t).astype(BF16)
        return dict(
            tokens=tokens,
            grads=grads,
            q=proj[:, :W],
            k=proj[:, W : 2 * W],
            v=proj[:, 2 * W :],
            q_t=proj_t[:W].astype(BF16),
            k_t=proj_t[W : 2 * W].astype(BF16),
            v_t=proj_t[2 * W : 3 * W].astype(BF16),
            gate_t=gate_t,
            d_mixed_t=d_mixed_t,
            d_att_t=d_att_t,
            d_att=d_att_t.T,
            att_h=[],
            dq_h=[],
            d_k=None,
            d_v=None,
        )

    lane = lax.broadcasted_iota(jnp.int32, (N, W), 1) // DH
    zero = jnp.zeros((N, W), BF16)

    def raw(col, h):
        rows = slice(h * DH, (h + 1) * DH)
        s = dot(col["k"][:, rows], col["q_t"][rows])
        d_probs = dot(col["v"][:, rows], col["d_att_t"][rows])
        return s, d_probs

    def head(col, h, bias, s, d_probs):
        own = lane == h
        rows = slice(h * DH, (h + 1) * DH)
        s = s * (SCALE * LOG2E) + bias
        e = jnp.exp2(s - jnp.max(s, axis=0, keepdims=True))
        probs = e * (1.0 / jnp.sum(e, axis=0, keepdims=True))
        probs_b = probs.astype(BF16)
        att_h = dot(col["v_t"][rows], probs_b)
        delta = jnp.sum(col["d_att_t"][rows].astype(F32) * att_h, axis=0, keepdims=True)
        d_s = probs * (d_probs - delta)
        d_sb = d_s.astype(BF16)
        col["att_h"].append(att_h)
        col["dq_h"].append(dot(col["k_t"][rows], d_sb))
        dk_h = dot(d_sb, jnp.where(own, col["q"], zero))
        dv_h = dot(probs_b, jnp.where(own, col["d_att"], zero))
        col["d_k"] = dk_h if h == 0 else col["d_k"] + dk_h
        col["d_v"] = dv_h if h == 0 else col["d_v"] + dv_h
        return d_s

    def finish(col):
        att_t = jnp.concatenate(col["att_h"], axis=0)
        gate_t = col["gate_t"]
        mixed_t = (gate_t * att_t).astype(BF16)
        d_gate_t = (col["d_mixed_t"] * att_t * gate_t * (1.0 - gate_t)).astype(BF16)
        d_q_t = (jnp.concatenate(col["dq_h"], axis=0) * SCALE).astype(BF16)
        d_proj = jnp.concatenate(
            [d_q_t.T, (col["d_k"] * SCALE).astype(BF16), col["d_v"].astype(BF16), d_gate_t.T],
            axis=1,
        )
        d_tokens = dot(d_proj, wt_ref[...])
        return dot(col["tokens"], d_proj, 0, 0), dot(mixed_t, col["grads"]), d_tokens

    def bias_of(h):
        return (
            jnp.concatenate(
                [
                    jnp.concatenate([cols_ref[4 * h + 2 * r], cols_ref[4 * h + 2 * r + 1]], axis=1)
                    for r in range(2)
                ],
                axis=0,
            ).astype(F32)
            * LOG2E
        )

    cols = [prepare(t) for t in range(4)]
    order = [(h, t) for h in range(2) for t in range(4)]
    ahead = [raw(cols[t], h) for h, t in order[:3]]
    for step, (h, t) in enumerate(order):
        s, d_probs = ahead.pop(0)
        if step + 3 < len(order):
            ahead.append(raw(cols[order[step + 3][1]], order[step + 3][0]))
        if t == 0:
            bias, total = bias_of(h), 0.0
        total = total + head(cols[t], h, bias, s, d_probs)
        if t == 3:
            for r in range(2):
                for m in range(2):
                    part = member(total[r * 128 : (r + 1) * 128], m).astype(BF16)
                    for half in range(2):
                        out_ref[8 * h + 4 * m + 2 * r + half] = part[
                            :, half * 128 : (half + 1) * 128
                        ]
    d_w, d_wout = 0.0, 0.0
    for t in range(4):
        part_w, part_wout, d_tokens = finish(cols[t])
        d_w, d_wout = d_w + part_w, d_wout + part_wout
        for r in range(2):
            for m in range(2):
                at = 16 + 8 * m + 4 * (t // 2) + 2 * r + t % 2
                out_ref[at] = member(d_tokens[r * 128 : (r + 1) * 128], m).astype(BF16)
    d_w = d_w.astype(BF16)
    for u in range(2):
        for block in range(2):
            out_ref[32 + 2 * u + block] = d_w[
                u * 64 : (u + 1) * 64, block * C : (block + 1) * C
            ]
    out_ref[36] = d_wout.astype(BF16)
    out_ref[37] = jnp.zeros((64, C), BF16)


def vmem(count):
    return [pl.BlockSpec(memory_space=pltpu.VMEM)] * count


def attention(cols, grads, w, w_t, w_out):
    return pl.pallas_call(
        attention_kernel,
        out_shape=jax.ShapeDtypeStruct((38, 64, C), BF16),
        in_specs=vmem(5),
        out_specs=vmem(1)[0],
        compiler_params=pltpu.CompilerParams(vmem_limit_bytes=24 << 20),
        cost_estimate=pl.CostEstimate(
            flops=900_000_000, bytes_accessed=3_000_000, transcendentals=600_000
        ),
    )(cols, grads, w, w_t, w_out)


def middle_kernel(back_ref, cells_ref, rows_ref, out_ref, d_xn_ref):
    def sums(row):
        return jnp.sum(back_ref[row].astype(F32), axis=0, keepdims=True)

    w_three = jnp.concatenate([rows_ref[:2]] * 3, axis=0).astype(BF16)
    d_wbias, d_gain = 0.0, 0.0
    for plane in range(8):
        m, cell = plane // 4, plane % 4
        xn, normed, _ = normalize(cells_ref[plane], rows_ref[2:3])
        owned = jnp.concatenate([sums(plane), sums(8 + plane)], axis=0)
        terms = [owned.astype(BF16)]
        left = owned - terms[0].astype(F32)
        terms.append(left.astype(BF16))
        terms.append((left - terms[1].astype(F32)).astype(BF16))
        three = jnp.concatenate(terms, axis=0)
        d_bias_x = dot(three, w_three, 0, 0)
        at = 16 + 8 * m + cell
        d_att_x = jnp.concatenate(
            [back_ref[at + 4 * j].astype(F32).reshape(8, 1, 8, C) for j in range(2)], axis=1
        )
        d_xn = d_att_x.reshape(128, C) + d_bias_x
        d_xn_ref[plane] = d_xn
        d_gain = d_gain + jnp.sum(d_xn * normed, axis=0, keepdims=True)
        parts = dot(three, xn)
        d_wbias = d_wbias + (parts[:2] + parts[2:4] + parts[4:])
    rows = jnp.concatenate([sums(row) for row in range(32, 37)] + [d_wbias, d_gain], axis=0)
    out_ref[...] = jnp.broadcast_to(rows[None], (DEV, 8, C)).astype(BF16)


def middle(back, cells, rows):
    return pl.pallas_call(
        middle_kernel,
        out_shape=(
            jax.ShapeDtypeStruct((DEV, 8, C), BF16),
            jax.ShapeDtypeStruct((8, DEV, C), F32),
        ),
        in_specs=vmem(3),
        out_specs=tuple(vmem(2)),
        compiler_params=pltpu.CompilerParams(vmem_limit_bytes=16 << 20),
    )(back, cells, rows)


def totals_kernel(planes_ref, w_ref, wout_ref, wbias_ref, gain_ref):
    scale = 1.0 / N

    def parts(row):
        plane = planes_ref[row].astype(F32) * scale
        return [member(plane, m) for m in range(2)]

    for u in range(2):
        for block in range(4):
            at = slice((block % 2) * W, (block % 2 + 1) * W)
            w_ref[u * 64 : (u + 1) * 64, block * C : (block + 1) * C] = jnp.concatenate(
                [part[:, at] for part in parts(2 * u + block // 2)], axis=1
            )
    for m, part in enumerate(parts(4)):
        wout_ref[m * W : (m + 1) * W] = part
    for h in range(2):
        for m, part in enumerate(parts(5 + h)):
            wbias_ref[2 * m + h : 2 * m + h + 1] = jnp.sum(part, axis=0, keepdims=True)
    gain_ref[...] = jnp.sum(planes_ref[7].astype(F32), axis=0, keepdims=True) * scale


def totals(planes):
    return pl.pallas_call(
        totals_kernel,
        out_shape=(
            jax.ShapeDtypeStruct((C, 4 * C), F32),
            jax.ShapeDtypeStruct((C, C), F32),
            jax.ShapeDtypeStruct((H, C), F32),
            jax.ShapeDtypeStruct((1, C), F32),
        ),
        in_specs=vmem(1),
        out_specs=tuple(vmem(4)),
        compiler_params=pltpu.CompilerParams(vmem_limit_bytes=8 << 20),
    )(planes)


def exchanged(blocks, axes=ROW):
    return lax.all_to_all(blocks, axes, split_axis=0, concat_axis=0, tiled=True)


def per_device(pair, out_grad, w_qkvg, w_out, w_bias, gain):
    sent = pack(pair, gain, w_bias)
    sent, pair, out_grad = lax.optimization_barrier((sent, pair, out_grad))
    mine = lax.axis_index("row_1")
    partner = [(0, 1), (1, 0)]
    cells = pair.reshape(2, 128, 2, C).transpose(0, 2, 1, 3).reshape(4, 128, C)
    grads = out_grad.reshape(128, 2, 2, C).transpose(2, 1, 0, 3).reshape(4, 128, C)

    def in_order(own, other):
        first, second = jnp.where(mine == 0, own, other), jnp.where(mine == 0, other, own)
        return jnp.concatenate([first, second], axis=0)

    other = lax.ppermute(jnp.concatenate([grads, cells], axis=0), "row_1", partner)
    grads = in_order(grads, other[:4]).reshape(4, N, C)
    pair_cells = in_order(cells, other[4:])
    rows = lax.dynamic_slice_in_dim(w_bias.T.astype(F32), 2 * mine, 2, axis=0)
    rows = jnp.concatenate([rows, gain[None]], axis=0)
    grads, pair_cells, rows = lax.optimization_barrier((grads, pair_cells, rows))
    w_own = lax.dynamic_index_in_dim(
        w_qkvg.reshape(C, 4, 2, W), mine, axis=2, keepdims=False
    ).reshape(C, 4 * W)
    wout_own = lax.dynamic_slice_in_dim(w_out, mine * W, W, axis=0)
    cols = exchanged(sent).transpose(1, 0, 2)
    planes = attention(cols, grads, w_own, w_own.T, wout_own)
    back = exchanged(planes.transpose(1, 0, 2).reshape(64, 19, 2, C), ("row_0", "row_2"))
    back = back.reshape(64, 38, C).transpose(1, 0, 2)
    last, d_xn = middle(back, pair_cells, rows)
    last, d_xn = lax.optimization_barrier((last, d_xn))
    arrived = exchanged(last)
    moved = lax.ppermute(jnp.where(mine == 0, d_xn[4:], d_xn[:4]).astype(BF16), "row_1", partner)

    moved, cells = lax.optimization_barrier((moved, cells))
    _, normed, inv_std = normalize(cells, gain)
    d_xn = jnp.where(mine == 0, d_xn[:4], d_xn[4:]) + moved.astype(F32)
    scaled = d_xn * gain
    d_pair = (
        inv_std
        * (
            scaled
            - jnp.mean(scaled, axis=-1, keepdims=True)
            - normed * jnp.mean(scaled * normed, axis=-1, keepdims=True)
        )
    ).astype(BF16)
    d_pair = d_pair.reshape(2, 2, 128, C).transpose(0, 2, 1, 3).reshape(2, N, C)
    d_w, d_wout, d_wbias, d_gain = totals(arrived.transpose(1, 0, 2))
    return d_pair, d_w, d_wout, d_wbias.T, d_gain[0]


def solution(mesh):
    split = Mesh(
        mesh.devices.reshape(mesh.shape["crop"], 8, 2, 8), ("crop", "row_0", "row_1", "row_2")
    )
    placed = (P(CROP_ROW, None, None), P("crop", ROW, None), P(), P(), P(), P())
    return jax.shard_map(
        per_device,
        mesh=split,
        in_specs=placed,
        out_specs=(
            P(CROP_ROW, None, None),
            P("crop", None),
            P("crop", None),
            P("crop", None),
            P("crop"),
        ),
        check_vma=False,
    )
```
